512 devices in a mesh: sa: 32 (over y, x, z_hi), tp: 16 (over z_lo, core).
Axes of the slice: x: 4, y: 4, z: 16 (z_hi: 2, z_lo: 8; z = z_hi * 8 + z_lo), core: 2. Of those that a mesh axis runs over, the one named last changes fastest.
Arguments:
- window: float32 [2, 2, 64, 32, 2048], P(None, None, 'sa', None, 'tp'), may hold values from -4 to 4
- damping: float32 [64, 32], P('sa'), may hold values from 0 to 1
- propagator: float32 [2, 32, 32], replicated, may hold values from -1 to 1, as said below
- coupling: float32 [32], replicated, may hold values from 0.5 to 1.5
Outputs:
- lesser_next: float32 [2, 64, 32, 2048], P(None, 'sa', None, 'tp')
The draws below stay inside these ranges and needn't reach their ends.
Inputs may be any that keep to these rules, and one draw needn't show every extreme that they name: `propagator`: a unitary matrix.
All inputs are finite; a program needn't handle non-finite values.
Results may differ from the reference program's by a relative error of at most 0.0079.
Values may be sent and summed in bfloat16 or wider, within the bound.
No kernel may reach another device: no remote copies, remote signals or barrier semaphores. Data moves between devices by JAX's collectives and lax.ppermute only.
A program may use at most 64 MiB of HBM per device.

```python
import math
import jax
import jax.numpy as jnp
from jax import lax

NO = 32
T_SIZE = 64


def draw_propagator(key, part):
    key_real = jax.random.fold_in(key, 11)
    key_imag = jax.random.fold_in(key, 12)
    sample_re = jax.random.normal(key_real, (NO, NO), jnp.float32)
    sample_im = jax.random.normal(key_imag, (NO, NO), jnp.float32)
    hermitian = ((sample_re + sample_re.T) * 0.5 + 1j * (sample_im - sample_im.T) * 0.5) * (1.5 / jnp.sqrt(NO * 1.0))
    identity = jnp.eye(NO, dtype=jnp.complex64)
    unitary = jnp.linalg.solve(identity + 0.5j * hermitian, identity - 0.5j * hermitian)
    return jnp.stack([jnp.real(unitary), jnp.imag(unitary)]).astype(jnp.float32)


def draw_damping(key, part):
    key_fast = jax.random.fold_in(key, 21)
    key_slow = jax.random.fold_in(key, 22)
    key_quick = jax.random.fold_in(key, 23)
    key_modulate = jax.random.fold_in(key, 24)
    key_spots = jax.random.fold_in(key, 25)
    key_factors = jax.random.fold_in(key, 26)
    fast_share = 0.5
    fast = jax.random.uniform(key_fast, (NO,), jnp.float32) < fast_share
    slow_rate = jax.random.uniform(key_slow, (NO,), jnp.float32, 0.05, 0.8) / T_SIZE
    quick_rate = jax.random.uniform(key_quick, (NO,), jnp.float32, 1.0 / 50.0, 1.0 / 30.0)
    relaxation_speeds = jnp.where(fast, quick_rate, slow_rate)
    forcing_envelope = jnp.exp(jax.random.uniform(key_modulate, (T_SIZE, 1), jnp.float32, -0.7, 0.7))
    excitation_locations = jax.random.randint(key_spots, (3,), 0, T_SIZE)
    amplitude_multipliers = jax.random.uniform(key_factors, (3,), jnp.float32, 0.6, 0.85)
    lattice_coordinates = jnp.arange(T_SIZE)[:, None]
    excitation_episodes = jnp.prod(jnp.where(lattice_coordinates == excitation_locations[None, :], amplitude_multipliers[None, :], 1.0), axis=1)
    return (jnp.exp(-relaxation_speeds[None, :] * forcing_envelope) * excitation_episodes[:, None]).astype(jnp.float32)


def block_scale(rng, extent, cuts, low, high):
    gain, own = 1.0, jax.random.fold_in(rng, 6)
    for dim, parts in cuts:
        steps = jnp.exp(jax.random.uniform(jax.random.fold_in(own, dim), (parts,), jnp.float32, low / len(cuts), high / len(cuts)))
        gain = gain * jnp.repeat(steps, extent[dim] // parts).reshape([-1 if axis == dim else 1 for axis in range(len(extent))])
    return gain


def centred(rng, shape, scale, reach, split=(), kind=jnp.bfloat16):
    drawn = jax.random.normal(rng, shape, jnp.float32) * scale
    if len(split) > 0:
        drawn = block_scale(rng, shape, split, -0.22, 0.18) * drawn
    return jnp.clip(drawn, min=-reach, max=reach).astype(kind)


def setup_inputs(seed: int = 0) -> dict:
    seeds = jax.random.split(jax.random.key(seed), 5)
    window = centred(seeds[0], (2, 2, T_SIZE, NO, T_SIZE * NO), 1.0, 4.0, ((2, 32), (4, 16)), jnp.float32)
    damping = draw_damping(jax.random.fold_in(seeds[4], 71), 0)
    propagator = draw_propagator(jax.random.fold_in(seeds[4], 71), 0)
    coupling = jnp.clip(jnp.exp(jax.random.uniform(seeds[3], (NO,), jnp.float32, math.log(0.5), math.log(1.5))), 0.5, 1.5)
    return dict(window=window, damping=damping, propagator=propagator, coupling=coupling)


highest = lax.Precision.HIGHEST

def spectral_self_energy(occupied_correlator, greater, coupling, column_tiles):
    factor = jnp.tile(coupling[:, None] * coupling[None, :], (1, column_tiles))
    less_re, less_im = (occupied_correlator[0], occupied_correlator[1])
    great_re, great_im = (greater[0], greater[1])
    lsquare_re = less_re * less_re - less_im * less_im
    lsquare_im = 2.0 * less_re * less_im
    gsquare_re = great_re * great_re - great_im * great_im
    gsquare_im = 2.0 * great_re * great_im
    sless_re = -factor * (lsquare_re * great_re + lsquare_im * great_im)
    sless_im = -factor * (lsquare_im * great_re - lsquare_re * great_im)
    sgreat_re = -factor * (gsquare_re * less_re + gsquare_im * less_im)
    sgreat_im = -factor * (gsquare_im * less_re - gsquare_re * less_im)
    return jnp.stack([sgreat_re - sless_re, sgreat_im - sless_im]).astype(jnp.bfloat16)

def complex_product(left_re, left_im, right_re, right_im):
    cosine_component = jnp.dot(left_re, right_re, precision=highest) - jnp.dot(left_im, right_im, precision=highest)
    imag_part = jnp.dot(left_re, right_im, precision=highest) + jnp.dot(left_im, right_re, precision=highest)
    return (cosine_component, imag_part)

def collision_term(spectral, history, weight_scale):
    width = spectral.shape[1] * spectral.shape[2]
    left_re = spectral[0].reshape(width, width)
    left_im = spectral[1].reshape(width, width)
    right_re = history[0].reshape(width, width)
    right_im = history[1].reshape(width, width)
    cosine_component = jnp.dot(left_re.astype(jnp.float32), right_re.astype(jnp.float32), preferred_element_type=jnp.float32) - jnp.dot(left_im.astype(jnp.float32), right_im.astype(jnp.float32), preferred_element_type=jnp.float32)
    imag_part = jnp.dot(left_re.astype(jnp.float32), right_im.astype(jnp.float32), preferred_element_type=jnp.float32) + jnp.dot(left_im.astype(jnp.float32), right_re.astype(jnp.float32), preferred_element_type=jnp.float32)
    return weight_scale * jnp.stack([cosine_component, imag_part]).reshape(history.shape)

def propagate(forcing, damping, propagator, initial):

    def advance(state, inputs):
        damp_row, force_row = inputs
        cosine_component, imag_part = complex_product(propagator[0], propagator[1], state[0], state[1])
        advanced = damp_row[None, :, None] * jnp.stack([cosine_component, imag_part]) + force_row
        return (advanced, advanced)
    last_state, produced = lax.scan(advance, initial, (damping, jnp.moveaxis(forcing, 1, 0)))
    return jnp.moveaxis(produced, 0, 1)

def reference(window, damping, propagator, coupling):
    occupied_correlator = window[0]
    greater = window[1]
    initial = occupied_correlator[:, 0]
    weight_scale = 1.0 / (T_SIZE * math.sqrt(NO))
    first_spectral = spectral_self_energy(occupied_correlator, greater, coupling, T_SIZE)
    first_term = collision_term(first_spectral, occupied_correlator.astype(jnp.bfloat16), weight_scale)
    predicted = propagate(first_term, damping, propagator, initial)
    second_spectral = spectral_self_energy(predicted, greater, coupling, T_SIZE)
    second_term = collision_term(second_spectral, predicted.astype(jnp.bfloat16), weight_scale)
    return propagate(0.5 * (first_term + second_term), damping, propagator, initial)
```

```python
import functools
import math

import jax
import jax.numpy as jnp
from jax import lax
from jax.experimental import pallas as pl
from jax.experimental.pallas import tpu as pltpu
from jax.sharding import Mesh
from jax.sharding import PartitionSpec as P

FIRST = ("y", "x", "zh")
SECOND = ("zm", "zq", "c")
PLANE = ("y", "x")
f32, bf16 = jnp.float32, jnp.bfloat16
VMEM = pl.BlockSpec(memory_space=pltpu.VMEM)
SMEM = pl.BlockSpec(memory_space=pltpu.SMEM)


def from_everyone(shard, axis):
    peers = lax.axis_size(axis)
    return lax.all_to_all(
        jnp.broadcast_to(shard[None], (peers, *shard.shape)), axis, 0, 0, tiled=True
    )


def swapped(shard, axis):
    return lax.ppermute(shard, axis, [(0, 1), (1, 0)])


def in_order(own, other, axis):
    first = lax.axis_index(axis) == 0
    return jnp.stack([jnp.where(first, own, other), jnp.where(first, other, own)])


def spectral(less_re, less_im, great_re, great_im, factor):
    lsquare_re = less_re * less_re - less_im * less_im
    lsquare_im = 2.0 * less_re * less_im
    gsquare_re = great_re * great_re - great_im * great_im
    gsquare_im = 2.0 * great_re * great_im
    real = (lsquare_re * great_re + lsquare_im * great_im) - (
        gsquare_re * less_re + gsquare_im * less_im
    )
    imag = (lsquare_im * great_re - lsquare_re * great_im) - (
        gsquare_im * less_re - gsquare_re * less_im
    )
    return factor * real, factor * imag


def dot(left, right):
    return jnp.dot(left, right, preferred_element_type=f32)


def row_times_column(core, own_ref, other_ref, y_ref, heights, acc_ref):
    acc_ref[...] = jnp.zeros_like(acc_ref)

    def step(q, carry):
        for s_ref, side in ((own_ref, core), (other_ref, 1 - core)):
            left, right = [], []
            for m in range(2):
                if heights == 2:
                    left.append(s_ref[q, :, m].reshape(256, 128))
                else:
                    left.append(s_ref[q, m])
                j = 8 * m + 2 * q + side
                right.append(
                    jnp.concatenate(
                        [
                            y_ref[j, :, 0:64].reshape(128, 128),
                            y_ref[j, :, 64:128].reshape(128, 128),
                        ],
                        axis=1,
                    )
                )
            acc_ref[...] += dot(jnp.concatenate(left, axis=1), jnp.concatenate(right, axis=0))
        return carry

    lax.fori_loop(0, 4, step, 0)


def first_collision(scale, where_ref, own_ref, other_ref, y_ref, out_ref, acc_ref):
    row_times_column(where_ref[2], own_ref, other_ref, y_ref, 2, acc_ref)
    for h in range(2):
        top, low = acc_ref[h * 128 : h * 128 + 64], acc_ref[h * 128 + 64 : h * 128 + 128]
        out_ref[h, 0:64] = (scale * (top[:, :128] - low[:, 128:])).astype(bf16)
        out_ref[h, 64:128] = (scale * (top[:, 128:] + low[:, :128])).astype(bf16)


def last_collision(scale, where_ref, own_ref, other_ref, y_ref, base_ref, out_ref, acc_ref):
    row_times_column(where_ref[2], own_ref, other_ref, y_ref, 1, acc_ref)
    top, low = acc_ref[0:64], acc_ref[64:128]
    out_ref[0] = base_ref[0:64] + (0.5 * scale) * (top[:, :128] - low[:, 128:])
    out_ref[1] = base_ref[64:128] + (0.5 * scale) * (top[:, 128:] + low[:, :128])


def halves(x):
    high = x.astype(bf16)
    return high, (x - high.astype(f32)).astype(bf16)


def long_product(left, right):
    lh, ll = left
    rh, rl = halves(right)
    return dot(
        jnp.concatenate([lh, lh, ll, ll], axis=1), jnp.concatenate([rh, rl, rh, rl], axis=0)
    )


def embedded(z):
    return jnp.concatenate([z, jnp.concatenate([-z[32:], z[:32]], axis=0)], axis=1)


def put_unit(z, at):
    row = lax.broadcasted_iota(jnp.int32, z.shape, 0)
    lane = lax.broadcasted_iota(jnp.int32, z.shape, 1)
    unit = jnp.where((row == lane - 32 * at) & (row < 32), 1.0, 0.0)
    return jnp.where(lane >= 32 * at, unit, z)


def lanes_from_zero(z, last):
    moved = jnp.concatenate([z[:, 32:], z[:, :32]], axis=1)
    row = lax.broadcasted_iota(jnp.int32, z.shape, 0)
    lane = lax.broadcasted_iota(jnp.int32, z.shape, 1)
    tail = jnp.where(row == lane - 224, 1.0, 0.0) if last else jnp.zeros_like(z)
    return jnp.where(lane >= 224, tail, moved)


def build_steps(damp_ref, u_ref, p_ref, q_ref, pc_ref, hc_ref, z_ref):
    unitary = embedded(u_ref[...])
    high, low = halves(unitary)

    def store(k, i, z):
        wide = lanes_from_zero(z, i == 7).astype(bf16)
        top, under = wide[:32], wide[32:]
        p_ref[k, i * 32 : i * 32 + 32, 0:256] = top
        p_ref[k, i * 32 : i * 32 + 32, 256:512] = -under
        p_ref[k, 256 + i * 32 : 288 + i * 32, 0:256] = under
        p_ref[k, 256 + i * 32 : 288 + i * 32, 256:512] = top
        first = embedded(z[:, :32]).astype(bf16)
        q_ref[k, i * 32 : i * 32 + 32] = first[:32]
        q_ref[k, 256 + i * 32 : 288 + i * 32] = first[32:]

    for k in range(8):
        start = jnp.concatenate([u_ref[...], jnp.zeros((64, 224), f32)], axis=1)
        z = put_unit(damp_ref[:, 8 * k : 8 * k + 1] * start, 1)
        z_ref[k] = z
        store(k, 0, z)
    for i in range(1, 8):
        for k in range(8):
            t = 8 * k + i
            z = damp_ref[:, t : t + 1] * long_product((high, low), z_ref[k])
            if i < 7:
                z = put_unit(z, i + 1)
            z_ref[k] = z
            store(k, i, z)

    w = None
    for k in range(8):
        whole = z_ref[k][:, :32]
        if k == 0:
            w = put_unit(jnp.concatenate([whole, jnp.zeros((64, 224), f32)], axis=1), 1)
        else:
            w = long_product(halves(embedded(whole)), w)
            if k < 7:
                w = put_unit(w, k + 1)
        wide = lanes_from_zero(w, k == 7).astype(bf16)
        top, under = wide[:32], wide[32:]
        pc_ref[k * 64 : k * 64 + 32, 0:256] = top
        pc_ref[k * 64 : k * 64 + 32, 256:512] = -under
        pc_ref[k * 64 + 32 : k * 64 + 64, 0:256] = under
        pc_ref[k * 64 + 32 : k * 64 + 64, 256:512] = top
        hc_ref[k * 64 : k * 64 + 64] = embedded(w[:, :32]).astype(bf16)


def predict(
    where_ref, force_ref, lg_ref, factor_ref, p_ref, q_ref, pc_ref, hc_ref,
    y_ref, t_ref, base_ref,
    loc_ref, s_ref, ends_ref, carry_ref, hom_ref,
):
    j, h = where_ref[0], where_ref[1]
    own_block, own_start = j // 2, pl.multiple_of((j % 2) * 128 + h * 64, 64)

    def block_of(ref, k, start):
        return jnp.concatenate(
            [
                ref[2 * k + u // 2, u % 2, start + 64 * part : start + 64 * part + 64]
                for part in range(2)
                for u in range(4)
            ],
            axis=0,
        )

    def local(k, _):
        x = dot(p_ref[k], block_of(force_ref, k, 0))
        loc_ref[k] = x
        ends_ref[0, k] = x[224:256].astype(bf16)
        ends_ref[1, k] = x[480:512].astype(bf16)
        return 0

    lax.fori_loop(0, 8, local, 0)
    initial = jnp.concatenate([lg_ref[0, 0, 0:32], lg_ref[0, 0, 64:96]], axis=0)
    hom = dot(hc_ref[...], initial)
    carry = dot(pc_ref[...], ends_ref[...].reshape(512, 128)) + hom
    hom_ref[0] = initial
    carry_ref[0] = initial
    for k in range(7):
        hom_ref[k + 1] = hom[k * 64 : k * 64 + 64].astype(bf16)
        carry_ref[k + 1] = carry[k * 64 : k * 64 + 64].astype(bf16)
    factor = factor_ref[...]

    def whole(k, _):
        x = loc_ref[k] + dot(q_ref[k], carry_ref[k])
        loc_ref[k] = x
        g = block_of(lg_ref, k, 128).astype(f32)
        real, imag = spectral(x[:256], x[256:], g[:256], g[256:], factor)
        s = jnp.concatenate([real, imag], axis=0).astype(bf16)
        s_ref[k] = s
        y = x.astype(bf16)
        for u in range(4):
            for part in range(2):
                y_ref[2 * k + u // 2, u % 2, 64 * part : 64 * part + 64] = y[
                    256 * part + 64 * u : 256 * part + 64 * u + 64
                ]
        last = jnp.concatenate([p_ref[k, 224:256], p_ref[k, 480:512]], axis=0)
        end = dot(last, s).astype(bf16)
        ends_ref[0, k] = end[:32]
        ends_ref[1, k] = end[32:]
        return 0

    lax.fori_loop(0, 8, whole, 0)
    carry = dot(pc_ref[...], ends_ref[...].reshape(512, 128))
    carry_ref[0] = jnp.zeros((64, 128), bf16)
    for k in range(7):
        carry_ref[k + 1] = carry[k * 64 : k * 64 + 64].astype(bf16)

    low = pl.multiple_of(own_start + 256, 64)

    def own(ref):
        return jnp.concatenate(
            [ref[own_block, pl.ds(own_start, 64)], ref[own_block, pl.ds(low, 64)]], axis=0
        )

    q_own = own(q_ref)
    t_ref[...] = (
        dot(own(p_ref), s_ref[own_block]) + dot(q_own, carry_ref[own_block])
    ).astype(bf16)
    base_ref[...] = 0.5 * (own(loc_ref) + dot(q_own, hom_ref[own_block]))


def call(kernel, outs, scratch, ins, flops, moved):
    return pl.pallas_call(
        kernel,
        out_shape=outs,
        in_specs=ins,
        out_specs=jax.tree.map(lambda _: VMEM, outs),
        scratch_shapes=scratch,
        cost_estimate=pl.CostEstimate(flops=flops, bytes_accessed=moved, transcendentals=0),
    )


def shape(*dims, kind=bf16):
    return jax.ShapeDtypeStruct(dims, kind)


def shards(window, damping, propagator, coupling):
    orbitals = coupling.shape[0]
    horizon = damping.shape[0] * lax.axis_size(FIRST)
    scale = 1.0 / (horizon * math.sqrt(orbitals))
    factor = jnp.tile(coupling[:, None] * coupling[None, :], (8, 4))
    window = window.reshape(2, 2, 64, 128)
    less, great = window[0], window[1]
    where = jnp.stack(
        [lax.axis_index(PLANE), lax.axis_index("zh"), lax.axis_index("c")]
    ).astype(jnp.int32)

    real, imag = spectral(less[0], less[1], great[0], great[1], factor[:64])
    s1 = jnp.concatenate([real, imag]).astype(bf16)

    d0 = damping.reshape(1, 64)
    high = lax.reduce_precision(d0, 8, 7)
    rest = d0 - high
    mid = lax.reduce_precision(rest, 8, 7)
    tail = rest - mid
    rows = jnp.concatenate([high, mid, tail, jnp.zeros_like(d0)], axis=1).reshape(2, 128)
    message = jnp.concatenate(
        [less.reshape(128, 128), great.reshape(128, 128), jnp.pad(rows, ((0, 14), (0, 0)))]
    ).astype(bf16)
    pair = in_order(message, swapped(message, "zh"), "zh")
    lg = from_everyone(pair, PLANE)

    s_rows = from_everyone(s1, ("zh", "zm"))
    s_rows = from_everyone(s_rows, "zq")
    s_other = swapped(s_rows, "c")
    s_rows = s_rows.reshape(4, 2, 2, 128, 128)
    s_other = s_other.reshape(4, 2, 2, 128, 128)

    c1 = call(
        functools.partial(first_collision, scale),
        shape(2, 128, 128),
        [pltpu.VMEM((256, 256), f32)],
        [SMEM, VMEM, VMEM, VMEM],
        2 * 256 * 256 * 2048,
        4 << 20,
    )(where, s_rows, s_other, lg)
    force = from_everyone(c1, PLANE)

    parts = lg[:, :, 256:258].astype(f32).reshape(32, 4, 64)
    damp = (parts[:, 0] + (parts[:, 1] + parts[:, 2])).reshape(64, 32)
    damp = jnp.tile(damp.T, (2, 1))
    steps, inflow, coarse, start = call(
        build_steps,
        (shape(8, 512, 512), shape(8, 512, 64), shape(512, 512), shape(512, 64)),
        [pltpu.VMEM((8, 64, 256), f32)],
        [VMEM, VMEM],
        64 * 2 * 64 * 256 * 256,
        6 << 20,
    )(damp, propagator.reshape(64, 32))

    y2, t2, base = call(
        predict,
        (shape(16, 2, 128, 128), shape(128, 128), shape(128, 128, kind=f32)),
        [
            pltpu.VMEM((8, 512, 128), f32),
            pltpu.VMEM((8, 512, 128), bf16),
            pltpu.VMEM((2, 8, 32, 128), bf16),
            pltpu.VMEM((8, 64, 128), bf16),
            pltpu.VMEM((8, 64, 128), bf16),
        ],
        [SMEM] + [VMEM] * 7,
        2 * 8 * 512 * 512 * 128 * 2,
        10 << 20,
    )(where, force, lg, factor, steps, inflow, coarse, start)

    t_rows = from_everyone(t2, "zm")
    t_rows = from_everyone(t_rows, "zq")
    t_other = swapped(t_rows, "c")
    out = call(
        functools.partial(last_collision, scale),
        shape(2, 64, 128, kind=f32),
        [pltpu.VMEM((128, 256), f32)],
        [SMEM, VMEM, VMEM, VMEM, VMEM],
        2 * 128 * 256 * 2048,
        2 << 20,
    )(where, t_rows, t_other, y2, base)
    return out.reshape(2, 2, orbitals, 128)


def solution(mesh):
    finer = Mesh(mesh.devices.reshape(4, 4, 2, 2, 4, 2), (*FIRST, *SECOND))
    placed = (P(None, None, FIRST, None, SECOND), P(FIRST, None), P(), P())
    return jax.shard_map(
        shards, mesh=finer, in_specs=placed, out_specs=P(None, FIRST, None, SECOND), check_vma=False
    )
```

```python
import functools
import math

import jax
import jax.numpy as jnp
from jax import lax
from jax.experimental import pallas as pl
from jax.experimental.pallas import tpu as pltpu
from jax.sharding import Mesh
from jax.sharding import PartitionSpec as P

FIRST = ("y", "x", "zh")
SECOND = ("zm", "zq", "c")
PLANE = ("y", "x")
f32, bf16 = jnp.float32, jnp.bfloat16
VMEM = pl.BlockSpec(memory_space=pltpu.VMEM)
SMEM = pl.BlockSpec(memory_space=pltpu.SMEM)


def from_everyone(shard, axis):
    peers = lax.axis_size(axis)
    return lax.all_to_all(
        jnp.broadcast_to(shard[None], (peers, *shard.shape)), axis, 0, 0, tiled=True
    )


def crossed(shard, axis, other):
    peers = lax.axis_size(axis)
    return lax.ppermute(shard, axis, [(k, k ^ other) for k in range(peers)])


def swapped(shard, axis):
    return crossed(shard, axis, 1)


def in_order(own, other, axis):
    first = lax.axis_index(axis) == 0
    return jnp.stack([jnp.where(first, own, other), jnp.where(first, other, own)])


def spectral(less_re, less_im, great_re, great_im, factor):
    lsquare_re = less_re * less_re - less_im * less_im
    lsquare_im = 2.0 * less_re * less_im
    gsquare_re = great_re * great_re - great_im * great_im
    gsquare_im = 2.0 * great_re * great_im
    real = (lsquare_re * great_re + lsquare_im * great_im) - (
        gsquare_re * less_re + gsquare_im * less_im
    )
    imag = (lsquare_im * great_re - lsquare_re * great_im) - (
        gsquare_im * less_re - gsquare_re * less_im
    )
    return factor * real, factor * imag


def dot(left, right):
    return jnp.dot(left, right, preferred_element_type=f32)


def row_times_column(pieces, y_ref, acc_ref):
    for n, (left, blocks) in enumerate(pieces):
        right = [
            jnp.concatenate(
                [y_ref[j, :, 0:64].reshape(128, 128), y_ref[j, :, 64:128].reshape(128, 128)],
                axis=1,
            )
            for j in blocks
        ]
        part = dot(jnp.concatenate(left, axis=1), jnp.concatenate(right, axis=0))
        if n == 0:
            acc_ref[...] = part
        else:
            acc_ref[...] += part


def first_collision(scale, where_ref, own_ref, other_ref, y_ref, out_ref, acc_ref):
    zm, zq, core = where_ref[2], where_ref[3], where_ref[4]
    pieces = [
        (
            [s_ref[d, e].reshape(256, 128) for e in range(2)],
            [8 * (zm ^ e) + 2 * (zq ^ d) + side for e in range(2)],
        )
        for s_ref, side in ((own_ref, core), (other_ref, 1 - core))
        for d in range(4)
    ]
    row_times_column(pieces, y_ref, acc_ref)
    for h in range(2):
        top, low = acc_ref[h * 128 : h * 128 + 64], acc_ref[h * 128 + 64 : h * 128 + 128]
        real = (scale * (top[:, :128] - low[:, 128:])).astype(bf16)
        imag = (scale * (top[:, 128:] + low[:, :128])).astype(bf16)
        for peer in range(16):
            out_ref[peer, h, 0:64] = real
            out_ref[peer, h, 64:128] = imag


def last_collision(scale, where_ref, own_ref, other_ref, y_ref, base_ref, out_ref, acc_ref):
    core = where_ref[4]
    pieces = [
        ([s_ref[2 * p + e] for e in range(2)], [4 * p + 2 * e + side for e in range(2)])
        for s_ref, side in ((own_ref, core), (other_ref, 1 - core))
        for p in range(4)
    ]
    row_times_column(pieces, y_ref, acc_ref)
    top, low = acc_ref[0:64], acc_ref[64:128]
    out_ref[0] = base_ref[0:64] + (0.5 * scale) * (top[:, :128] - low[:, 128:])
    out_ref[1] = base_ref[64:128] + (0.5 * scale) * (top[:, 128:] + low[:, :128])


def halves(x):
    high = x.astype(bf16)
    return high, (x - high.astype(f32)).astype(bf16)


def long_product(left, right):
    lh, ll = left
    rh, rl = halves(right)
    return dot(
        jnp.concatenate([lh, lh, ll, ll], axis=1), jnp.concatenate([rh, rl, rh, rl], axis=0)
    )


def embedded(z):
    return jnp.concatenate([z, jnp.concatenate([-z[32:], z[:32]], axis=0)], axis=1)


def put_unit(z, at):
    row = lax.broadcasted_iota(jnp.int32, z.shape, 0)
    lane = lax.broadcasted_iota(jnp.int32, z.shape, 1)
    unit = jnp.where((row == lane - 32 * at) & (row < 32), 1.0, 0.0)
    return jnp.where(lane >= 32 * at, unit, z)


def lanes_from_zero(z, last):
    moved = jnp.concatenate([z[:, 32:], z[:, :32]], axis=1)
    row = lax.broadcasted_iota(jnp.int32, z.shape, 0)
    lane = lax.broadcasted_iota(jnp.int32, z.shape, 1)
    tail = jnp.where(row == lane - 224, 1.0, 0.0) if last else jnp.zeros_like(z)
    return jnp.where(lane >= 224, tail, moved)


def build_steps(damp_ref, u_ref, p_ref, q_ref, pc_ref, hc_ref, z_ref):
    left = halves(embedded(u_ref[...]))

    def store(k, i, z):
        high, low = halves(lanes_from_zero(z, i == 7))
        first_high, first_low = halves(z[:, :32])
        first = jnp.concatenate([first_high, first_high, first_low], axis=1)
        for part in range(2):
            start = 256 * part + 32 * i
            rows, to = slice(32 * part, 32 * part + 32), slice(start, start + 32)
            p_ref[k, to, 0:256] = high[rows]
            p_ref[k, to, 256:512] = low[rows]
            q_ref[k, to] = first[rows]

    for k in range(8):
        start = jnp.concatenate([u_ref[...], jnp.zeros((64, 224), f32)], axis=1)
        z = put_unit(damp_ref[:, 8 * k : 8 * k + 1] * start, 1)
        z_ref[k] = z
        store(k, 0, z)
    for i in range(1, 8):
        for k in range(8):
            t = 8 * k + i
            z = damp_ref[:, t : t + 1] * long_product(left, z_ref[k])
            if i < 7:
                z = put_unit(z, i + 1)
            z_ref[k] = z
            store(k, i, z)

    w = None
    for k in range(8):
        whole = z_ref[k][:, :32]
        if k == 0:
            w = put_unit(jnp.concatenate([whole, jnp.zeros((64, 224), f32)], axis=1), 1)
        else:
            w = long_product(halves(embedded(whole)), w)
            if k < 7:
                w = put_unit(w, k + 1)
        high, low = halves(lanes_from_zero(w, k == 7))
        rows = slice(k * 64, k * 64 + 64)
        pc_ref[rows, 0:256] = high
        pc_ref[rows, 256:512] = high
        pc_ref[rows, 512:768] = low
        hc_ref[rows] = jnp.concatenate(halves(w[:, :32]), axis=1)


def predict(
    where_ref, force_ref, lg_ref, factor_ref, p_ref, q_ref, pc_ref, hc_ref,
    y_ref, t_ref, base_ref,
    f_ref, s_ref, ends_ref, carry_ref, hom_ref, x_ref,
):
    j, h = where_ref[0], where_ref[1]
    own_block, own_start = j // 2, pl.multiple_of((j % 2) * 128 + h * 64, 64)
    own_low = pl.multiple_of(own_start + 256, 64)

    def block_of(ref, k, start):
        return jnp.concatenate(
            [
                jnp.concatenate(
                    [
                        ref[2 * k + u // 2, u % 2, start + 64 * part : start + 64 * part + 64]
                        for u in range(4)
                    ],
                    axis=0,
                )
                for part in range(2)
            ],
            axis=1,
        )

    def parts(product):
        rows = product.shape[0] // 2
        top, low = product[:rows], product[rows:]
        return top[:, :128] - low[:, 128:], top[:, 128:] + low[:, :128]

    def twice(x):
        return jnp.concatenate([x, x], axis=0)

    def last_rows(k):
        return jnp.concatenate([p_ref[k, 224:256], p_ref[k, 480:512]], axis=0)

    def put_end(k, source):
        real, imag = parts(dot(last_rows(k), twice(source)))
        high, low = halves(jnp.concatenate([real, imag], axis=1))
        ends_ref[0, k], ends_ref[1, k], ends_ref[2, k] = high, low, high

    def coarse():
        return dot(pc_ref[...], ends_ref[...].reshape(768, 256))

    def rows_of(product, k):
        part = product[k * 64 : k * 64 + 64]
        return jnp.concatenate(parts(part), axis=1)

    def triple(x):
        high, low = halves(x)
        return jnp.concatenate([high, low, high], axis=0)

    for k in range(8):
        source = block_of(force_ref, k, 0)
        f_ref[k] = source
        put_end(k, source)
    initial = jnp.concatenate([lg_ref[0, 0, 0:32], lg_ref[0, 0, 64:96]], axis=1)
    hom = dot(hc_ref[...], twice(initial))
    carry = coarse() + hom
    hom_ref[0] = carry_ref[0] = triple(initial.astype(f32))
    for k in range(7):
        hom_ref[k + 1] = triple(rows_of(hom, k))
        carry_ref[k + 1] = triple(rows_of(carry, k))
    factor = factor_ref[...]

    def whole(k, _):
        real, imag = parts(dot(p_ref[k], twice(f_ref[k])) + dot(q_ref[k], carry_ref[k]))
        x_ref[k, 0:256], x_ref[k, 256:512] = real, imag
        g = block_of(lg_ref, k, 128).astype(f32)
        spectral_re, spectral_im = spectral(real, imag, g[:, :128], g[:, 128:], factor)
        s = jnp.concatenate([spectral_re, spectral_im], axis=1).astype(bf16)
        s_ref[k] = s
        for part, y in enumerate((real.astype(bf16), imag.astype(bf16))):
            for u in range(4):
                y_ref[2 * k + u // 2, u % 2, 64 * part : 64 * part + 64] = y[64 * u : 64 * u + 64]
        put_end(k, s)
        return 0

    lax.fori_loop(0, 8, whole, 0)
    carry = coarse()
    carry_ref[0] = jnp.zeros((96, 256), bf16)
    for k in range(7):
        carry_ref[k + 1] = triple(rows_of(carry, k))

    def own(ref):
        return jnp.concatenate(
            [ref[own_block, pl.ds(own_start, 64)], ref[own_block, pl.ds(own_low, 64)]], axis=0
        )

    q_own = own(q_ref)
    real, imag = parts(dot(own(p_ref), twice(s_ref[own_block])) + dot(q_own, carry_ref[own_block]))
    t_ref[0:64], t_ref[64:128] = real.astype(bf16), imag.astype(bf16)
    real, imag = parts(dot(q_own, hom_ref[own_block]))
    base = own(x_ref)
    base_ref[0:64] = 0.5 * (base[0:64] + real)
    base_ref[64:128] = 0.5 * (base[64:128] + imag)


def call(kernel, outs, scratch, ins, flops, moved):
    return pl.pallas_call(
        kernel,
        out_shape=outs,
        in_specs=ins,
        out_specs=jax.tree.map(lambda _: VMEM, outs),
        scratch_shapes=scratch,
        compiler_params=pltpu.CompilerParams(vmem_limit_bytes=24 << 20),
        cost_estimate=pl.CostEstimate(flops=flops, bytes_accessed=moved, transcendentals=0),
    )


def shape(*dims, kind=bf16):
    return jax.ShapeDtypeStruct(dims, kind)


def shards(window, damping, propagator, coupling):
    orbitals = coupling.shape[0]
    horizon = damping.shape[0] * lax.axis_size(FIRST)
    scale = 1.0 / (horizon * math.sqrt(orbitals))
    factor = jnp.tile(coupling[:, None] * coupling[None, :], (8, 4))
    window = window.reshape(2, 2, 64, 128)
    less, great = window[0], window[1]
    where = jnp.stack(
        [lax.axis_index(axis) for axis in (PLANE, "zh", "zm", "zq", "c")]
    ).astype(jnp.int32)

    real, imag = spectral(less[0], less[1], great[0], great[1], factor[:64])
    s1 = jnp.concatenate([real, imag]).astype(bf16)

    d0 = damping.reshape(1, 64)
    high = lax.reduce_precision(d0, 8, 7)
    rest = d0 - high
    mid = lax.reduce_precision(rest, 8, 7)
    tail = rest - mid
    rows = jnp.concatenate([high, mid, tail, jnp.zeros_like(d0)], axis=1).reshape(2, 128)
    message = jnp.concatenate(
        [
            less.reshape(128, 128).astype(bf16),
            great.reshape(128, 128).astype(bf16),
            jnp.pad(rows.astype(bf16), ((0, 14), (0, 0))),
            s1,
        ]
    )
    pair = in_order(message, swapped(message, "zh"), "zh")
    lg = from_everyone(pair[:, :272], PLANE)

    s_rows = pair[:, 272:]
    s_rows = jnp.stack([s_rows, swapped(s_rows, "zm")])
    s_rows = jnp.stack([s_rows] + [crossed(s_rows, "zq", d) for d in (1, 2, 3)])
    s_other = swapped(s_rows, "c")

    c1 = call(
        functools.partial(first_collision, scale),
        shape(16, 2, 128, 128),
        [pltpu.VMEM((256, 256), f32)],
        [SMEM, VMEM, VMEM, VMEM],
        2 * 256 * 256 * 2048,
        4 << 20,
    )(where, s_rows, s_other, lg)
    force = lax.all_to_all(c1, PLANE, 0, 0, tiled=True)

    parts = lg[:, :, 256:258].astype(f32).reshape(32, 4, 64)
    damp = (parts[:, 0] + (parts[:, 1] + parts[:, 2])).reshape(64, 32)
    damp = jnp.tile(damp.T, (2, 1))
    steps, inflow, coarse, start = call(
        build_steps,
        (shape(8, 512, 512), shape(8, 512, 96), shape(512, 768), shape(512, 64)),
        [pltpu.VMEM((8, 64, 256), f32)],
        [VMEM, VMEM],
        64 * 2 * 64 * 256 * 256,
        6 << 20,
    )(damp, propagator.reshape(64, 32))

    y2, t2, base = call(
        predict,
        (shape(16, 2, 128, 128), shape(128, 128), shape(128, 128, kind=f32)),
        [
            pltpu.VMEM((8, 256, 256), bf16),
            pltpu.VMEM((8, 256, 256), bf16),
            pltpu.VMEM((3, 8, 32, 256), bf16),
            pltpu.VMEM((8, 96, 256), bf16),
            pltpu.VMEM((8, 96, 256), bf16),
            pltpu.VMEM((8, 512, 128), f32),
        ],
        [SMEM] + [VMEM] * 7,
        2 * 8 * 512 * 512 * 128 * 2,
        10 << 20,
    )(where, force, lg, factor, steps, inflow, coarse, start)

    t_rows = from_everyone(t2, ("zm", "zq"))
    t_other = swapped(t_rows, "c")
    out = call(
        functools.partial(last_collision, scale),
        shape(2, 64, 128, kind=f32),
        [pltpu.VMEM((128, 256), f32)],
        [SMEM, VMEM, VMEM, VMEM, VMEM],
        2 * 128 * 256 * 2048,
        2 << 20,
    )(where, t_rows, t_other, y2, base)
    return out.reshape(2, 2, orbitals, 128)


def solution(mesh):
    finer = Mesh(mesh.devices.reshape(4, 4, 2, 2, 4, 2), (*FIRST, *SECOND))
    placed = (P(None, None, FIRST, None, SECOND), P(FIRST, None), P(), P())
    return jax.shard_map(
        shards, mesh=finer, in_specs=placed, out_specs=P(None, FIRST, None, SECOND), check_vma=False
    )
```

```python
import functools
import math

import jax
import jax.numpy as jnp
from jax import lax
from jax.experimental import pallas as pl
from jax.experimental.pallas import tpu as pltpu
from jax.sharding import Mesh
from jax.sharding import PartitionSpec as P

FIRST = ("y", "x", "zh")
SECOND = ("zm", "zq", "c")
PLANE = ("y", "x")
f32, bf16 = jnp.float32, jnp.bfloat16
VMEM = pl.BlockSpec(memory_space=pltpu.VMEM)
SMEM = pl.BlockSpec(memory_space=pltpu.SMEM)
HBM = pl.BlockSpec(memory_space=pltpu.HBM)


def from_everyone(shard, axis):
    peers = lax.axis_size(axis)
    return lax.all_to_all(
        jnp.broadcast_to(shard[None], (peers, *shard.shape)), axis, 0, 0, tiled=True
    )


def crossed(shard, axis, other):
    peers = lax.axis_size(axis)
    return lax.ppermute(shard, axis, [(k, k ^ other) for k in range(peers)])


def swapped(shard, axis):
    return crossed(shard, axis, 1)


def in_order(own, other, axis):
    first = lax.axis_index(axis) == 0
    return jnp.stack([jnp.where(first, own, other), jnp.where(first, other, own)])


def couplings(row, times):
    wide = jnp.broadcast_to(row, (32, 32))
    at_row = lax.broadcasted_iota(jnp.int32, (32, 32), 0)
    at_lane = lax.broadcasted_iota(jnp.int32, (32, 32), 1)
    column = jnp.sum(jnp.where(at_row == at_lane, wide, 0.0), axis=1, keepdims=True)
    tile = jnp.concatenate([column * wide] * 4, axis=1)
    return jnp.concatenate([tile] * times, axis=0)


def spectral(less_re, less_im, great_re, great_im, factor):
    lsquare_re = less_re * less_re - less_im * less_im
    lsquare_im = 2.0 * less_re * less_im
    gsquare_re = great_re * great_re - great_im * great_im
    gsquare_im = 2.0 * great_re * great_im
    real = (lsquare_re * great_re + lsquare_im * great_im) - (
        gsquare_re * less_re + gsquare_im * less_im
    )
    imag = (lsquare_im * great_re - lsquare_re * great_im) - (
        gsquare_im * less_re - gsquare_re * less_im
    )
    return factor * real, factor * imag


def dot(left, right):
    return jnp.dot(left, right, preferred_element_type=f32)


def compose(window_ref, damp_ref, coupling_ref, out_ref):
    fields = [[window_ref[which, part] for part in range(2)] for which in range(2)]
    for which in range(2):
        for part in range(2):
            start = 128 * which + 64 * part
            out_ref[start : start + 64] = fields[which][part].astype(bf16)
    damp = damp_ref[...]
    high = damp.astype(bf16).astype(f32)
    mid = (damp - high).astype(bf16).astype(f32)
    low = damp - high - mid
    rows = jnp.concatenate([high, mid, low, jnp.zeros_like(low)], axis=1)
    out_ref[256:272] = jnp.concatenate([rows, jnp.zeros((14, 128), f32)], axis=0).astype(bf16)
    real, imag = spectral(*fields[0], *fields[1], couplings(coupling_ref[...], 2))
    out_ref[272:336], out_ref[336:400] = real.astype(bf16), imag.astype(bf16)


def row_times_column(pieces, y_ref, acc_ref):
    for n, (left, blocks) in enumerate(pieces):
        right = [
            jnp.concatenate(
                [y_ref[j, :, 0:64].reshape(128, 128), y_ref[j, :, 64:128].reshape(128, 128)],
                axis=1,
            )
            for j in blocks
        ]
        part = dot(jnp.concatenate(left, axis=1), jnp.concatenate(right, axis=0))
        if n == 0:
            acc_ref[...] = part
        else:
            acc_ref[...] += part


def first_collision(scale, where_ref, own_ref, other_ref, y_ref, out_ref, acc_ref):
    zm, zq, core = where_ref[2], where_ref[3], where_ref[4]
    pieces = [
        (
            [s_ref[d, e].reshape(256, 128) for e in range(2)],
            [8 * (zm ^ e) + 2 * (zq ^ d) + side for e in range(2)],
        )
        for s_ref, side in ((own_ref, core), (other_ref, 1 - core))
        for d in range(4)
    ]
    row_times_column(pieces, y_ref, acc_ref)
    for h in range(2):
        top, low = acc_ref[h * 128 : h * 128 + 64], acc_ref[h * 128 + 64 : h * 128 + 128]
        real = (scale * (top[:, :128] - low[:, 128:])).astype(bf16)
        imag = (scale * (top[:, 128:] + low[:, :128])).astype(bf16)
        for peer in range(16):
            out_ref[peer, h, 0:64] = real
            out_ref[peer, h, 64:128] = imag


def last_collision(scale, where_ref, own_ref, other_ref, y_ref, base_ref, out_ref, acc_ref):
    zm, core = where_ref[2], where_ref[4]
    pieces = [
        ([s_ref[q, e] for e in range(2)], [8 * (zm ^ e) + 2 * q + side for e in range(2)])
        for s_ref, side in ((own_ref, core), (other_ref, 1 - core))
        for q in range(4)
    ]
    row_times_column(pieces, y_ref, acc_ref)
    top, low = acc_ref[0:64], acc_ref[64:128]
    out_ref[0] = base_ref[0:64] + (0.5 * scale) * (top[:, :128] - low[:, 128:])
    out_ref[1] = base_ref[64:128] + (0.5 * scale) * (top[:, 128:] + low[:, :128])


def halves(x):
    high = x.astype(bf16)
    return high, (x - high.astype(f32)).astype(bf16)


def long_product(left, right):
    lh, ll = left
    rh, rl = halves(right)
    return dot(
        jnp.concatenate([lh, lh, ll, ll], axis=1), jnp.concatenate([rh, rl, rh, rl], axis=0)
    )


def embedded(z):
    return jnp.concatenate([z, jnp.concatenate([-z[32:], z[:32]], axis=0)], axis=1)


def put_unit(z, at):
    row = lax.broadcasted_iota(jnp.int32, z.shape, 0)
    lane = lax.broadcasted_iota(jnp.int32, z.shape, 1)
    unit = jnp.where((row == lane - 32 * at) & (row < 32), 1.0, 0.0)
    return jnp.where(lane >= 32 * at, unit, z)


def lanes_from_zero(z, last):
    moved = jnp.concatenate([z[:, 32:], z[:, :32]], axis=1)
    row = lax.broadcasted_iota(jnp.int32, z.shape, 0)
    lane = lax.broadcasted_iota(jnp.int32, z.shape, 1)
    tail = jnp.where(row == lane - 224, 1.0, 0.0) if last else jnp.zeros_like(z)
    return jnp.where(lane >= 224, tail, moved)


def build_steps(damp_ref, u_ref, out_hbm, p_ref, last_ref, pc_ref, z_ref, sems):
    copies = [
        pltpu.make_async_copy(p_ref.at[k], out_hbm.at[k, 0:512, 0:640], sems.at[k])
        for k in range(8)
    ]
    copies.append(pltpu.make_async_copy(last_ref, out_hbm.at[:, 512:576, 0:512], sems.at[8]))
    copies.append(pltpu.make_async_copy(pc_ref, out_hbm.at[:, 576:640, 0:896], sems.at[9]))
    left = halves(embedded(u_ref[...]))

    def store(k, i, z):
        high, low = halves(lanes_from_zero(z, i == 7))
        first_high, first_low = halves(z[:, :32])
        first = jnp.concatenate([first_high, first_high, first_low], axis=1)
        for part in range(2):
            start = 256 * part + 32 * i
            rows, to = slice(32 * part, 32 * part + 32), slice(start, start + 32)
            p_ref[k, to, 0:256] = high[rows]
            p_ref[k, to, 256:512] = low[rows]
            p_ref[k, to, 512:608] = first[rows]
            if i == 7:
                last_ref[k, rows, 0:256] = high[rows]
                last_ref[k, rows, 256:512] = low[rows]

    for k in range(8):
        start = jnp.concatenate([u_ref[...], jnp.zeros((64, 224), f32)], axis=1)
        z = put_unit(damp_ref[:, 8 * k : 8 * k + 1] * start, 1)
        z_ref[k] = z
        store(k, 0, z)
    for i in range(1, 8):
        for k in range(8):
            t = 8 * k + i
            z = damp_ref[:, t : t + 1] * long_product(left, z_ref[k])
            if i < 7:
                z = put_unit(z, i + 1)
            z_ref[k] = z
            store(k, i, z)
            if i == 7:
                copies[k].start()
    copies[8].start()

    w = None
    for k in range(8):
        whole = z_ref[k][:, :32]
        if k == 0:
            w = put_unit(jnp.concatenate([whole, jnp.zeros((64, 224), f32)], axis=1), 1)
        else:
            w = long_product(halves(embedded(whole)), w)
            if k < 7:
                w = put_unit(w, k + 1)
        high, low = halves(lanes_from_zero(w, k == 7))
        pc_ref[k, :, 0:256] = high
        pc_ref[k, :, 256:512] = high
        pc_ref[k, :, 512:768] = low
        pc_ref[k, :, 768:832] = jnp.concatenate(halves(w[:, :32]), axis=1)
    copies[9].start()
    for copy in copies:
        copy.wait()


def predict(
    where_ref, force_ref, lg_ref, coupling_ref, plan_hbm,
    y_ref, t_ref, base_ref,
    p_ref, last_ref, pc_ref, f_ref, s_ref, ends_ref, carry_ref, hom_ref, x_ref, sems,
):
    copies = [
        pltpu.make_async_copy(plan_hbm.at[:, 512:576, 0:512], last_ref, sems.at[8]),
        pltpu.make_async_copy(plan_hbm.at[:, 576:640, 0:896], pc_ref, sems.at[9]),
    ]

    def fetch(k):
        return pltpu.make_async_copy(
            plan_hbm.at[k, 0:512, 0:640], p_ref.at[k], sems.at[k]
        )

    for copy in copies + [fetch(k) for k in range(8)]:
        copy.start()

    j, h = where_ref[0], where_ref[1]
    own_block, own_start = j // 2, pl.multiple_of((j % 2) * 128 + h * 64, 64)
    own_low = pl.multiple_of(own_start + 256, 64)

    def block_of(ref, k, start):
        return jnp.concatenate(
            [
                jnp.concatenate(
                    [
                        ref[2 * k + u // 2, u % 2, start + 64 * part : start + 64 * part + 64]
                        for u in range(4)
                    ],
                    axis=0,
                )
                for part in range(2)
            ],
            axis=1,
        )

    def parts(product):
        rows = product.shape[0] // 2
        top, low = product[:rows], product[rows:]
        return top[:, :128] - low[:, 128:], top[:, 128:] + low[:, :128]

    def twice(x):
        return jnp.concatenate([x, x], axis=0)

    def put_end(k, source):
        real, imag = parts(dot(last_ref[k], twice(source)))
        high, low = halves(jnp.concatenate([real, imag], axis=1))
        ends_ref[0, k], ends_ref[1, k], ends_ref[2, k] = high, low, high

    def coarse():
        return dot(pc_ref[:, :, 0:768].reshape(512, 768), ends_ref[...].reshape(768, 256))

    def rows_of(product, k):
        part = product[k * 64 : k * 64 + 64]
        return jnp.concatenate(parts(part), axis=1)

    def triple(x):
        high, low = halves(x)
        return jnp.concatenate([high, low, high], axis=0)

    for k in range(8):
        f_ref[k] = block_of(force_ref, k, 0)
    copies[0].wait()
    for k in range(8):
        put_end(k, f_ref[k])
    copies[1].wait()
    initial = jnp.concatenate([lg_ref[0, 0, 0:32], lg_ref[0, 0, 64:96]], axis=1)
    hom = dot(pc_ref[:, :, 768:832].reshape(512, 64), twice(initial))
    carry = coarse() + hom
    hom_ref[0] = carry_ref[0] = triple(initial.astype(f32))
    for k in range(7):
        hom_ref[k + 1] = triple(rows_of(hom, k))
        carry_ref[k + 1] = triple(rows_of(carry, k))
    factor = couplings(coupling_ref[...], 8)

    def whole(k, _):
        fetch(k).wait()
        source = jnp.concatenate([f_ref[k], f_ref[k], carry_ref[k]], axis=0)
        real, imag = parts(dot(p_ref[k, :, 0:608], source))
        x_ref[k, 0:256], x_ref[k, 256:512] = real, imag
        g = block_of(lg_ref, k, 128).astype(f32)
        spectral_re, spectral_im = spectral(real, imag, g[:, :128], g[:, 128:], factor)
        s = jnp.concatenate([spectral_re, spectral_im], axis=1).astype(bf16)
        s_ref[k] = s
        for part, y in enumerate((real.astype(bf16), imag.astype(bf16))):
            for u in range(4):
                y_ref[2 * k + u // 2, u % 2, 64 * part : 64 * part + 64] = y[64 * u : 64 * u + 64]
        put_end(k, s)
        return 0

    lax.fori_loop(0, 8, whole, 0)
    carry = coarse()
    carry_ref[0] = jnp.zeros((96, 256), bf16)
    for k in range(7):
        carry_ref[k + 1] = triple(rows_of(carry, k))

    def own(ref):
        return jnp.concatenate(
            [ref[own_block, pl.ds(own_start, 64)], ref[own_block, pl.ds(own_low, 64)]], axis=0
        )

    p_own, s_own = own(p_ref), s_ref[own_block]
    source = jnp.concatenate([s_own, s_own, carry_ref[own_block]], axis=0)
    real, imag = parts(dot(p_own[:, 0:608], source))
    t_ref[0:64], t_ref[64:128] = real.astype(bf16), imag.astype(bf16)
    real, imag = parts(dot(p_own[:, 512:608], hom_ref[own_block]))
    base = own(x_ref)
    base_ref[0:64] = 0.5 * (base[0:64] + real)
    base_ref[64:128] = 0.5 * (base[64:128] + imag)


def call(kernel, outs, scratch, ins, flops, moved, grant=24, place=VMEM):
    return pl.pallas_call(
        kernel,
        out_shape=outs,
        in_specs=ins,
        out_specs=jax.tree.map(lambda _: place, outs),
        scratch_shapes=scratch,
        compiler_params=pltpu.CompilerParams(vmem_limit_bytes=grant << 20),
        cost_estimate=pl.CostEstimate(flops=flops, bytes_accessed=moved, transcendentals=0),
    )


def shape(*dims, kind=bf16):
    return jax.ShapeDtypeStruct(dims, kind)


def shards(window, damping, propagator, coupling):
    orbitals = coupling.shape[0]
    horizon = damping.shape[0] * lax.axis_size(FIRST)
    scale = 1.0 / (horizon * math.sqrt(orbitals))
    where = jnp.stack(
        [lax.axis_index(axis) for axis in (PLANE, "zh", "zm", "zq", "c")]
    ).astype(jnp.int32)

    strength = coupling.reshape(1, 32)
    message = call(
        compose,
        shape(400, 128),
        [],
        [VMEM, VMEM, VMEM],
        40 * 64 * 128,
        400 << 10,
    )(window.reshape(2, 2, 64, 128), damping, strength)
    pair = in_order(message, swapped(message, "zh"), "zh")
    lg = from_everyone(pair[:, :272], PLANE)

    s_rows = pair[:, 272:]
    s_rows = jnp.stack([s_rows, swapped(s_rows, "zm")])
    s_rows = jnp.stack([s_rows] + [crossed(s_rows, "zq", d) for d in (1, 2, 3)])
    s_other = swapped(s_rows, "c")

    c1 = call(
        functools.partial(first_collision, scale),
        shape(16, 2, 128, 128),
        [pltpu.VMEM((256, 256), f32)],
        [SMEM, VMEM, VMEM, VMEM],
        2 * 256 * 256 * 2048,
        4 << 20,
    )(where, s_rows, s_other, lg)
    force = lax.all_to_all(c1, PLANE, 0, 0, tiled=True)

    parts = lg[:, :, 256:258].reshape(64, 128).astype(f32)
    damp = parts[:, 0:32] + (parts[:, 32:64] + parts[:, 64:96])
    damp = jnp.tile(damp.T, (2, 1))
    plan = call(
        build_steps,
        shape(8, 640, 1024),
        [
            pltpu.VMEM((8, 512, 640), bf16),
            pltpu.VMEM((8, 64, 512), bf16),
            pltpu.VMEM((8, 64, 896), bf16),
            pltpu.VMEM((8, 64, 256), f32),
            pltpu.SemaphoreType.DMA((10,)),
        ],
        [VMEM, VMEM],
        64 * 2 * 64 * 256 * 256,
        6 << 20,
        54,
        HBM,
    )(damp, propagator.reshape(64, 32))

    y2, t2, base = call(
        predict,
        (shape(16, 2, 128, 128), shape(128, 128), shape(128, 128, kind=f32)),
        [
            pltpu.VMEM((8, 512, 640), bf16),
            pltpu.VMEM((8, 64, 512), bf16),
            pltpu.VMEM((8, 64, 896), bf16),
            pltpu.VMEM((8, 256, 256), bf16),
            pltpu.VMEM((8, 256, 256), bf16),
            pltpu.VMEM((3, 8, 32, 256), bf16),
            pltpu.VMEM((8, 96, 256), bf16),
            pltpu.VMEM((8, 96, 256), bf16),
            pltpu.VMEM((8, 512, 128), f32),
            pltpu.SemaphoreType.DMA((10,)),
        ],
        [SMEM] + [VMEM] * 3 + [HBM],
        2 * 8 * 512 * 512 * 128 * 2,
        10 << 20,
        44,
    )(where, force, lg, strength, plan)

    t_rows = from_everyone(jnp.stack([t2, swapped(t2, "zm")]), "zq")
    t_other = swapped(t_rows, "c")
    out = call(
        functools.partial(last_collision, scale),
        shape(2, 64, 128, kind=f32),
        [pltpu.VMEM((128, 256), f32)],
        [SMEM, VMEM, VMEM, VMEM, VMEM],
        2 * 128 * 256 * 2048,
        2 << 20,
    )(where, t_rows, t_other, y2, base)
    return out.reshape(2, 2, orbitals, 128)


def solution(mesh):
    finer = Mesh(mesh.devices.reshape(4, 4, 2, 2, 4, 2), (*FIRST, *SECOND))
    placed = (P(None, None, FIRST, None, SECOND), P(FIRST, None), P(), P())
    return jax.shard_map(
        shards, mesh=finer, in_specs=placed, out_specs=P(None, FIRST, None, SECOND), check_vma=False
    )
```

```python
import functools
import math

import jax
import jax.numpy as jnp
from jax import lax
from jax.experimental import pallas as pl
from jax.experimental.pallas import tpu as pltpu
from jax.sharding import Mesh
from jax.sharding import PartitionSpec as P

FIRST = ("y", "x", "zh")
SECOND = ("zm", "zq", "c")
PLANE = ("y", "x")
f32, bf16 = jnp.float32, jnp.bfloat16
VMEM = pl.BlockSpec(memory_space=pltpu.VMEM)
SMEM = pl.BlockSpec(memory_space=pltpu.SMEM)
HBM = pl.BlockSpec(memory_space=pltpu.HBM)


def from_everyone(shard, axis):
    peers = lax.axis_size(axis)
    return lax.all_to_all(
        jnp.broadcast_to(shard[None], (peers, *shard.shape)), axis, 0, 0, tiled=True
    )


def swapped(shard, axis):
    return lax.ppermute(shard, axis, [(0, 1), (1, 0)])


def couplings(row, times):
    wide = jnp.broadcast_to(row, (32, 32))
    at_row = lax.broadcasted_iota(jnp.int32, (32, 32), 0)
    at_lane = lax.broadcasted_iota(jnp.int32, (32, 32), 1)
    column = jnp.sum(jnp.where(at_row == at_lane, wide, 0.0), axis=1, keepdims=True)
    tile = jnp.concatenate([column * wide] * 4, axis=1)
    return jnp.concatenate([tile] * times, axis=0)


def spectral(less_re, less_im, great_re, great_im, factor):
    lsquare_re = less_re * less_re - less_im * less_im
    lsquare_im = 2.0 * less_re * less_im
    gsquare_re = great_re * great_re - great_im * great_im
    gsquare_im = 2.0 * great_re * great_im
    real = (lsquare_re * great_re + lsquare_im * great_im) - (
        gsquare_re * less_re + gsquare_im * less_im
    )
    imag = (lsquare_im * great_re - lsquare_re * great_im) - (
        gsquare_im * less_re - gsquare_re * less_im
    )
    return factor * real, factor * imag


def dot(left, right):
    return jnp.dot(left, right, preferred_element_type=f32)


def compose(window_ref, damp_ref, coupling_ref, out_ref):
    fields = [[window_ref[which, part] for part in range(2)] for which in range(2)]
    for which in range(2):
        for part in range(2):
            start = 128 * which + 64 * part
            out_ref[start : start + 64] = fields[which][part].astype(bf16)
    damp = damp_ref[...]
    high = damp.astype(bf16).astype(f32)
    mid = (damp - high).astype(bf16).astype(f32)
    low = damp - high - mid
    rows = jnp.concatenate([high, mid, low, jnp.zeros_like(low)], axis=1)
    out_ref[256:272] = jnp.concatenate([rows, jnp.zeros((14, 128), f32)], axis=0).astype(bf16)
    real, imag = spectral(*fields[0], *fields[1], couplings(coupling_ref[...], 2))
    out_ref[272:336], out_ref[336:400] = real.astype(bf16), imag.astype(bf16)


def row_times_column(pieces, y_ref, acc_ref):
    for n, (left, blocks) in enumerate(pieces):
        right = [
            jnp.concatenate(
                [y_ref[j, :, 0:64].reshape(128, 128), y_ref[j, :, 64:128].reshape(128, 128)],
                axis=1,
            )
            for j in blocks
        ]
        part = dot(jnp.concatenate(left, axis=1), jnp.concatenate(right, axis=0))
        if n == 0:
            acc_ref[...] = part
        else:
            acc_ref[...] += part


def first_collision(scale, where_ref, own_ref, other_ref, y_ref, out_ref, acc_ref):
    core = where_ref[2]
    pieces = [
        (
            [s_ref[q, m].reshape(256, 128) for m in range(2)],
            [8 * m + 2 * q + side for m in range(2)],
        )
        for s_ref, side in ((own_ref, core), (other_ref, 1 - core))
        for q in range(4)
    ]
    row_times_column(pieces, y_ref, acc_ref)
    for h in range(2):
        top, low = acc_ref[h * 128 : h * 128 + 64], acc_ref[h * 128 + 64 : h * 128 + 128]
        real = (scale * (top[:, :128] - low[:, 128:])).astype(bf16)
        imag = (scale * (top[:, 128:] + low[:, :128])).astype(bf16)
        for peer in range(16):
            out_ref[peer, h, 0:64] = real
            out_ref[peer, h, 64:128] = imag


def last_collision(scale, where_ref, own_ref, other_ref, y_ref, base_ref, out_ref, acc_ref):
    core = where_ref[2]
    pieces = [
        ([s_ref[q, m] for m in range(2)], [8 * m + 2 * q + side for m in range(2)])
        for s_ref, side in ((own_ref, core), (other_ref, 1 - core))
        for q in range(4)
    ]
    row_times_column(pieces, y_ref, acc_ref)
    top, low = acc_ref[0:64], acc_ref[64:128]
    out_ref[0] = base_ref[0:64] + (0.5 * scale) * (top[:, :128] - low[:, 128:])
    out_ref[1] = base_ref[64:128] + (0.5 * scale) * (top[:, 128:] + low[:, :128])


def halves(x):
    high = x.astype(bf16)
    return high, (x - high.astype(f32)).astype(bf16)


def long_product(left, right):
    lh, ll = left
    rh, rl = halves(right)
    return dot(
        jnp.concatenate([lh, lh, ll, ll], axis=1), jnp.concatenate([rh, rl, rh, rl], axis=0)
    )


def embedded(z):
    return jnp.concatenate([z, jnp.concatenate([-z[32:], z[:32]], axis=0)], axis=1)


def put_unit(z, at):
    row = lax.broadcasted_iota(jnp.int32, z.shape, 0)
    lane = lax.broadcasted_iota(jnp.int32, z.shape, 1)
    unit = jnp.where((row == lane - 32 * at) & (row < 32), 1.0, 0.0)
    return jnp.where(lane >= 32 * at, unit, z)


def lanes_from_zero(z, last):
    moved = jnp.concatenate([z[:, 32:], z[:, :32]], axis=1)
    row = lax.broadcasted_iota(jnp.int32, z.shape, 0)
    lane = lax.broadcasted_iota(jnp.int32, z.shape, 1)
    tail = jnp.where(row == lane - 224, 1.0, 0.0) if last else jnp.zeros_like(z)
    return jnp.where(lane >= 224, tail, moved)


def build_steps(damp_ref, u_ref, out_hbm, p_ref, last_ref, pc_ref, z_ref, sems):
    copies = [
        pltpu.make_async_copy(p_ref.at[k], out_hbm.at[k, 0:512, 0:640], sems.at[k])
        for k in range(8)
    ]
    copies.append(pltpu.make_async_copy(last_ref, out_hbm.at[:, 512:576, 0:512], sems.at[8]))
    copies.append(pltpu.make_async_copy(pc_ref, out_hbm.at[:, 576:640, 0:896], sems.at[9]))
    left = halves(embedded(u_ref[...]))

    def store(k, i, z):
        high, low = halves(lanes_from_zero(z, i == 7))
        first_high, first_low = halves(z[:, :32])
        first = jnp.concatenate([first_high, first_high, first_low], axis=1)
        for part in range(2):
            start = 256 * part + 32 * i
            rows, to = slice(32 * part, 32 * part + 32), slice(start, start + 32)
            p_ref[k, to, 0:256] = high[rows]
            p_ref[k, to, 256:512] = low[rows]
            p_ref[k, to, 512:608] = first[rows]
            if i == 7:
                last_ref[k, rows, 0:256] = high[rows]
                last_ref[k, rows, 256:512] = low[rows]

    for k in range(8):
        start = jnp.concatenate([u_ref[...], jnp.zeros((64, 224), f32)], axis=1)
        z = put_unit(damp_ref[:, 8 * k : 8 * k + 1] * start, 1)
        z_ref[k] = z
        store(k, 0, z)
    for i in range(1, 8):
        for k in range(8):
            t = 8 * k + i
            z = damp_ref[:, t : t + 1] * long_product(left, z_ref[k])
            if i < 7:
                z = put_unit(z, i + 1)
            z_ref[k] = z
            store(k, i, z)
            if i == 7:
                copies[k].start()
    copies[8].start()

    w = None
    for k in range(8):
        whole = z_ref[k][:, :32]
        if k == 0:
            w = put_unit(jnp.concatenate([whole, jnp.zeros((64, 224), f32)], axis=1), 1)
        else:
            w = long_product(halves(embedded(whole)), w)
            if k < 7:
                w = put_unit(w, k + 1)
        high, low = halves(lanes_from_zero(w, k == 7))
        pc_ref[k, :, 0:256] = high
        pc_ref[k, :, 256:512] = high
        pc_ref[k, :, 512:768] = low
        pc_ref[k, :, 768:832] = jnp.concatenate(halves(w[:, :32]), axis=1)
    copies[9].start()
    for copy in copies:
        copy.wait()


def predict(
    where_ref, force_ref, lg_ref, coupling_ref, plan_hbm,
    y_ref, t_ref, base_ref,
    p_ref, last_ref, pc_ref, f_ref, s_ref, ends_ref, carry_ref, hom_ref, x_ref, sems,
):
    copies = [
        pltpu.make_async_copy(plan_hbm.at[:, 512:576, 0:512], last_ref, sems.at[8]),
        pltpu.make_async_copy(plan_hbm.at[:, 576:640, 0:896], pc_ref, sems.at[9]),
    ]

    def fetch(k):
        return pltpu.make_async_copy(
            plan_hbm.at[k, 0:512, 0:640], p_ref.at[k], sems.at[k]
        )

    for copy in copies + [fetch(k) for k in range(8)]:
        copy.start()

    j, h = where_ref[0], where_ref[1]
    own_block, own_start = j // 2, pl.multiple_of((j % 2) * 128 + h * 64, 64)
    own_low = pl.multiple_of(own_start + 256, 64)

    def block_of(ref, k, start):
        return jnp.concatenate(
            [
                jnp.concatenate(
                    [
                        ref[2 * k + u // 2, u % 2, start + 64 * part : start + 64 * part + 64]
                        for u in range(4)
                    ],
                    axis=0,
                )
                for part in range(2)
            ],
            axis=1,
        )

    def parts(product):
        rows = product.shape[0] // 2
        top, low = product[:rows], product[rows:]
        return top[:, :128] - low[:, 128:], top[:, 128:] + low[:, :128]

    def twice(x):
        return jnp.concatenate([x, x], axis=0)

    def put_end(k, source):
        real, imag = parts(dot(last_ref[k], twice(source)))
        high, low = halves(jnp.concatenate([real, imag], axis=1))
        ends_ref[0, k], ends_ref[1, k], ends_ref[2, k] = high, low, high

    def coarse():
        return dot(pc_ref[:, :, 0:768].reshape(512, 768), ends_ref[...].reshape(768, 256))

    def rows_of(product, k):
        part = product[k * 64 : k * 64 + 64]
        return jnp.concatenate(parts(part), axis=1)

    def triple(x):
        high, low = halves(x)
        return jnp.concatenate([high, low, high], axis=0)

    for k in range(8):
        f_ref[k] = block_of(force_ref, k, 0)
    copies[0].wait()
    for k in range(8):
        put_end(k, f_ref[k])
    copies[1].wait()
    initial = jnp.concatenate([lg_ref[0, 0, 0:32], lg_ref[0, 0, 64:96]], axis=1)
    hom = dot(pc_ref[:, :, 768:832].reshape(512, 64), twice(initial))
    carry = coarse() + hom
    hom_ref[0] = carry_ref[0] = triple(initial.astype(f32))
    for k in range(7):
        hom_ref[k + 1] = triple(rows_of(hom, k))
        carry_ref[k + 1] = triple(rows_of(carry, k))
    factor = couplings(coupling_ref[...], 8)

    def whole(k, _):
        fetch(k).wait()
        source = jnp.concatenate([f_ref[k], f_ref[k], carry_ref[k]], axis=0)
        real, imag = parts(dot(p_ref[k, :, 0:608], source))
        x_ref[k, 0:256], x_ref[k, 256:512] = real, imag
        g = block_of(lg_ref, k, 128).astype(f32)
        spectral_re, spectral_im = spectral(real, imag, g[:, :128], g[:, 128:], factor)
        s = jnp.concatenate([spectral_re, spectral_im], axis=1).astype(bf16)
        s_ref[k] = s
        for part, y in enumerate((real.astype(bf16), imag.astype(bf16))):
            for u in range(4):
                y_ref[2 * k + u // 2, u % 2, 64 * part : 64 * part + 64] = y[64 * u : 64 * u + 64]
        put_end(k, s)
        return 0

    lax.fori_loop(0, 8, whole, 0)
    carry = coarse()
    carry_ref[0] = jnp.zeros((96, 256), bf16)
    for k in range(7):
        carry_ref[k + 1] = triple(rows_of(carry, k))

    def own(ref):
        return jnp.concatenate(
            [ref[own_block, pl.ds(own_start, 64)], ref[own_block, pl.ds(own_low, 64)]], axis=0
        )

    p_own, s_own = own(p_ref), s_ref[own_block]
    source = jnp.concatenate([s_own, s_own, carry_ref[own_block]], axis=0)
    real, imag = parts(dot(p_own[:, 0:608], source))
    t_ref[0:64], t_ref[64:128] = real.astype(bf16), imag.astype(bf16)
    real, imag = parts(dot(p_own[:, 512:608], hom_ref[own_block]))
    base = own(x_ref)
    base_ref[0:64] = 0.5 * (base[0:64] + real)
    base_ref[64:128] = 0.5 * (base[64:128] + imag)


def call(kernel, outs, scratch, ins, flops, moved, grant=24, place=VMEM):
    return pl.pallas_call(
        kernel,
        out_shape=outs,
        in_specs=ins,
        out_specs=jax.tree.map(lambda _: place, outs),
        scratch_shapes=scratch,
        compiler_params=pltpu.CompilerParams(vmem_limit_bytes=grant << 20),
        cost_estimate=pl.CostEstimate(flops=flops, bytes_accessed=moved, transcendentals=0),
    )


def shape(*dims, kind=bf16):
    return jax.ShapeDtypeStruct(dims, kind)


def shards(window, damping, propagator, coupling):
    orbitals = coupling.shape[0]
    horizon = damping.shape[0] * lax.axis_size(FIRST)
    scale = 1.0 / (horizon * math.sqrt(orbitals))
    where = jnp.stack([lax.axis_index(axis) for axis in (PLANE, "zh", "c")]).astype(jnp.int32)

    strength = coupling.reshape(1, 32)
    message = call(
        compose,
        shape(400, 128),
        [],
        [VMEM, VMEM, VMEM],
        40 * 64 * 128,
        400 << 10,
    )(window.reshape(2, 2, 64, 128), damping, strength)
    pair = lax.all_gather(message, "zh")
    lg = from_everyone(pair[:, :272], PLANE)

    s_rows = lax.all_gather(pair[:, 272:], "zm")
    s_rows = lax.all_gather(s_rows, "zq")
    s_other = swapped(s_rows, "c")

    c1 = call(
        functools.partial(first_collision, scale),
        shape(16, 2, 128, 128),
        [pltpu.VMEM((256, 256), f32)],
        [SMEM, VMEM, VMEM, VMEM],
        2 * 256 * 256 * 2048,
        4 << 20,
    )(where, s_rows, s_other, lg)
    force = lax.all_to_all(c1, PLANE, 0, 0, tiled=True)

    parts = lg[:, :, 256:258].reshape(64, 128).astype(f32)
    damp = parts[:, 0:32] + (parts[:, 32:64] + parts[:, 64:96])
    damp = jnp.tile(damp.T, (2, 1))
    plan = call(
        build_steps,
        shape(8, 640, 1024),
        [
            pltpu.VMEM((8, 512, 640), bf16),
            pltpu.VMEM((8, 64, 512), bf16),
            pltpu.VMEM((8, 64, 896), bf16),
            pltpu.VMEM((8, 64, 256), f32),
            pltpu.SemaphoreType.DMA((10,)),
        ],
        [VMEM, VMEM],
        64 * 2 * 64 * 256 * 256,
        6 << 20,
        54,
        HBM,
    )(damp, propagator.reshape(64, 32))

    y2, t2, base = call(
        predict,
        (shape(16, 2, 128, 128), shape(128, 128), shape(128, 128, kind=f32)),
        [
            pltpu.VMEM((8, 512, 640), bf16),
            pltpu.VMEM((8, 64, 512), bf16),
            pltpu.VMEM((8, 64, 896), bf16),
            pltpu.VMEM((8, 256, 256), bf16),
            pltpu.VMEM((8, 256, 256), bf16),
            pltpu.VMEM((3, 8, 32, 256), bf16),
            pltpu.VMEM((8, 96, 256), bf16),
            pltpu.VMEM((8, 96, 256), bf16),
            pltpu.VMEM((8, 512, 128), f32),
            pltpu.SemaphoreType.DMA((10,)),
        ],
        [SMEM] + [VMEM] * 3 + [HBM],
        2 * 8 * 512 * 512 * 128 * 2,
        10 << 20,
        44,
    )(where, force, lg, strength, plan)

    t_rows = lax.all_gather(lax.all_gather(t2, "zm"), "zq")
    t_other = swapped(t_rows, "c")
    out = call(
        functools.partial(last_collision, scale),
        shape(2, 64, 128, kind=f32),
        [pltpu.VMEM((128, 256), f32)],
        [SMEM, VMEM, VMEM, VMEM, VMEM],
        2 * 128 * 256 * 2048,
        2 << 20,
    )(where, t_rows, t_other, y2, base)
    return out.reshape(2, 2, orbitals, 128)


def solution(mesh):
    finer = Mesh(mesh.devices.reshape(4, 4, 2, 2, 4, 2), (*FIRST, *SECOND))
    placed = (P(None, None, FIRST, None, SECOND), P(FIRST, None), P(), P())
    return jax.shard_map(
        shards, mesh=finer, in_specs=placed, out_specs=P(None, FIRST, None, SECOND), check_vma=False
    )
```

```python
import functools
import math

import jax
import jax.numpy as jnp
from jax import lax
from jax.experimental import pallas as pl
from jax.experimental.pallas import tpu as pltpu
from jax.sharding import Mesh
from jax.sharding import PartitionSpec as P

FIRST = ("y", "x", "zh")
SECOND = ("zm", "zq", "c")
PLANE = ("y", "x")
f32, bf16 = jnp.float32, jnp.bfloat16
VMEM = pl.BlockSpec(memory_space=pltpu.VMEM)
SMEM = pl.BlockSpec(memory_space=pltpu.SMEM)
HBM = pl.BlockSpec(memory_space=pltpu.HBM)


def from_everyone(shard, axis):
    peers = lax.axis_size(axis)
    return lax.all_to_all(
        jnp.broadcast_to(shard[None], (peers, *shard.shape)), axis, 0, 0, tiled=True
    )


def swapped(shard, axis):
    return lax.ppermute(shard, axis, [(0, 1), (1, 0)])


def couplings(row, times):
    wide = jnp.broadcast_to(row, (32, 32))
    at_row = lax.broadcasted_iota(jnp.int32, (32, 32), 0)
    at_lane = lax.broadcasted_iota(jnp.int32, (32, 32), 1)
    column = jnp.sum(jnp.where(at_row == at_lane, wide, 0.0), axis=1, keepdims=True)
    tile = jnp.concatenate([column * wide] * 4, axis=1)
    return jnp.concatenate([tile] * times, axis=0)


def spectral(less_re, less_im, great_re, great_im, factor):
    lsquare_re = less_re * less_re - less_im * less_im
    lsquare_im = 2.0 * less_re * less_im
    gsquare_re = great_re * great_re - great_im * great_im
    gsquare_im = 2.0 * great_re * great_im
    real = (lsquare_re * great_re + lsquare_im * great_im) - (
        gsquare_re * less_re + gsquare_im * less_im
    )
    imag = (lsquare_im * great_re - lsquare_re * great_im) - (
        gsquare_im * less_re - gsquare_re * less_im
    )
    return factor * real, factor * imag


def dot(left, right):
    return jnp.dot(left, right, preferred_element_type=f32)


def compose(window_ref, damp_ref, coupling_ref, out_ref):
    fields = [[window_ref[which, part] for part in range(2)] for which in range(2)]
    for which in range(2):
        for part in range(2):
            start = 128 * which + 64 * part
            out_ref[start : start + 64] = fields[which][part].astype(bf16)
    damp = damp_ref[...]
    high = damp.astype(bf16).astype(f32)
    mid = (damp - high).astype(bf16).astype(f32)
    low = damp - high - mid
    rows = jnp.concatenate([high, mid, low, jnp.zeros_like(low)], axis=1)
    out_ref[256:272] = jnp.concatenate([rows, jnp.zeros((14, 128), f32)], axis=0).astype(bf16)
    real, imag = spectral(*fields[0], *fields[1], couplings(coupling_ref[...], 2))
    out_ref[272:336], out_ref[336:400] = real.astype(bf16), imag.astype(bf16)


def row_times_column(pieces, y_ref, acc_ref):
    for n, (left, blocks) in enumerate(pieces):
        right = [
            jnp.concatenate(
                [y_ref[j, :, 0:64].reshape(128, 128), y_ref[j, :, 64:128].reshape(128, 128)],
                axis=1,
            )
            for j in blocks
        ]
        part = dot(jnp.concatenate(left, axis=1), jnp.concatenate(right, axis=0))
        if n == 0:
            acc_ref[...] = part
        else:
            acc_ref[...] += part


def first_collision(scale, where_ref, own_ref, other_ref, y_ref, out_ref, acc_ref):
    core = where_ref[2]
    pieces = [
        (
            [s_ref[q, m].reshape(256, 128) for m in range(2)],
            [8 * m + 2 * q + side for m in range(2)],
        )
        for s_ref, side in ((own_ref, core), (other_ref, 1 - core))
        for q in range(4)
    ]
    row_times_column(pieces, y_ref, acc_ref)
    for h in range(2):
        top, low = acc_ref[h * 128 : h * 128 + 64], acc_ref[h * 128 + 64 : h * 128 + 128]
        real = (scale * (top[:, :128] - low[:, 128:])).astype(bf16)
        imag = (scale * (top[:, 128:] + low[:, :128])).astype(bf16)
        for peer in range(16):
            out_ref[peer, h, 0:64] = real
            out_ref[peer, h, 64:128] = imag


def last_collision(scale, where_ref, own_ref, other_ref, y_ref, base_ref, out_ref, acc_ref):
    core = where_ref[2]
    pieces = [
        ([s_ref[q, m] for m in range(2)], [8 * m + 2 * q + side for m in range(2)])
        for s_ref, side in ((own_ref, core), (other_ref, 1 - core))
        for q in range(4)
    ]
    row_times_column(pieces, y_ref, acc_ref)
    top, low = acc_ref[0:64], acc_ref[64:128]
    out_ref[0] = base_ref[0:64] + (0.5 * scale) * (top[:, :128] - low[:, 128:])
    out_ref[1] = base_ref[64:128] + (0.5 * scale) * (top[:, 128:] + low[:, :128])


def halves(x):
    high = x.astype(bf16)
    return high, (x - high.astype(f32)).astype(bf16)


def long_product(left, right):
    lh, ll = left
    rh, rl = halves(right)
    return dot(
        jnp.concatenate([lh, lh, ll, ll], axis=1), jnp.concatenate([rh, rl, rh, rl], axis=0)
    )


def embedded(z):
    return jnp.concatenate([z, jnp.concatenate([-z[32:], z[:32]], axis=0)], axis=1)


def put_unit(z, at):
    row = lax.broadcasted_iota(jnp.int32, z.shape, 0)
    lane = lax.broadcasted_iota(jnp.int32, z.shape, 1)
    unit = jnp.where((row == lane - 32 * at) & (row < 32), 1.0, 0.0)
    return jnp.where(lane >= 32 * at, unit, z)


def lanes_from_zero(z, last):
    moved = jnp.concatenate([z[:, 32:], z[:, :32]], axis=1)
    row = lax.broadcasted_iota(jnp.int32, z.shape, 0)
    lane = lax.broadcasted_iota(jnp.int32, z.shape, 1)
    tail = jnp.where(row == lane - 224, 1.0, 0.0) if last else jnp.zeros_like(z)
    return jnp.where(lane >= 224, tail, moved)


def build_steps(damp_ref, u_ref, out_hbm, p_ref, last_ref, pc_ref, z_ref, sems):
    copies = [
        pltpu.make_async_copy(p_ref.at[k], out_hbm.at[k, 0:512, 0:640], sems.at[k])
        for k in range(8)
    ]
    copies.append(pltpu.make_async_copy(last_ref, out_hbm.at[:, 512:576, 0:512], sems.at[8]))
    copies.append(pltpu.make_async_copy(pc_ref, out_hbm.at[:, 576:640, 0:896], sems.at[9]))
    left = halves(embedded(u_ref[...]))

    def store(k, i, z):
        high, low = halves(lanes_from_zero(z, i == 7))
        first_high, first_low = halves(z[:, :32])
        first = jnp.concatenate([first_high, first_high, first_low], axis=1)
        for part in range(2):
            start = 256 * part + 32 * i
            rows, to = slice(32 * part, 32 * part + 32), slice(start, start + 32)
            p_ref[k, to, 0:256] = high[rows]
            p_ref[k, to, 256:512] = low[rows]
            p_ref[k, to, 512:608] = first[rows]
            if i == 7:
                last_ref[k, rows, 0:256] = high[rows]
                last_ref[k, rows, 256:512] = low[rows]

    for k in range(8):
        start = jnp.concatenate([u_ref[...], jnp.zeros((64, 224), f32)], axis=1)
        z = put_unit(damp_ref[:, 8 * k : 8 * k + 1] * start, 1)
        z_ref[k] = z
        store(k, 0, z)
    for i in range(1, 8):
        for k in range(8):
            t = 8 * k + i
            z = damp_ref[:, t : t + 1] * long_product(left, z_ref[k])
            if i < 7:
                z = put_unit(z, i + 1)
            z_ref[k] = z
            store(k, i, z)
            if i == 7:
                copies[k].start()
    copies[8].start()

    w = None
    for k in range(8):
        whole = z_ref[k][:, :32]
        if k == 0:
            w = put_unit(jnp.concatenate([whole, jnp.zeros((64, 224), f32)], axis=1), 1)
        else:
            w = long_product(halves(embedded(whole)), w)
            if k < 7:
                w = put_unit(w, k + 1)
        high, low = halves(lanes_from_zero(w, k == 7))
        pc_ref[k, :, 0:256] = high
        pc_ref[k, :, 256:512] = high
        pc_ref[k, :, 512:768] = low
        pc_ref[k, :, 768:832] = jnp.concatenate(halves(w[:, :32]), axis=1)
    copies[9].start()
    for copy in copies:
        copy.wait()


def predict(
    where_ref, force_ref, lg_ref, coupling_ref, plan_hbm,
    y_ref, t_ref, base_ref,
    p_ref, last_ref, pc_ref, f_ref, s_ref, ends_ref, carry_ref, hom_ref, x_ref, sems,
):
    copies = [
        pltpu.make_async_copy(plan_hbm.at[:, 512:576, 0:512], last_ref, sems.at[8]),
        pltpu.make_async_copy(plan_hbm.at[:, 576:640, 0:896], pc_ref, sems.at[9]),
    ]

    def fetch(k):
        return pltpu.make_async_copy(
            plan_hbm.at[k, 0:512, 0:640], p_ref.at[k], sems.at[k]
        )

    for copy in copies + [fetch(k) for k in range(8)]:
        copy.start()

    j, h = where_ref[0], where_ref[1]
    own_block, own_start = j // 2, pl.multiple_of((j % 2) * 128 + h * 64, 64)
    own_low = pl.multiple_of(own_start + 256, 64)

    def block_of(ref, k, start):
        return jnp.concatenate(
            [
                jnp.concatenate(
                    [
                        ref[2 * k + u // 2, u % 2, start + 64 * part : start + 64 * part + 64]
                        for u in range(4)
                    ],
                    axis=0,
                )
                for part in range(2)
            ],
            axis=1,
        )

    def parts(product):
        rows = product.shape[0] // 2
        top, low = product[:rows], product[rows:]
        return top[:, :128] - low[:, 128:], top[:, 128:] + low[:, :128]

    def twice(x):
        return jnp.concatenate([x, x], axis=0)

    def put_end(k, source):
        real, imag = parts(dot(last_ref[k], twice(source)))
        high, low = halves(jnp.concatenate([real, imag], axis=1))
        ends_ref[0, k], ends_ref[1, k], ends_ref[2, k] = high, low, high

    def coarse():
        return dot(pc_ref[:, :, 0:768].reshape(512, 768), ends_ref[...].reshape(768, 256))

    def rows_of(product, k):
        part = product[k * 64 : k * 64 + 64]
        return jnp.concatenate(parts(part), axis=1)

    def triple(x):
        high, low = halves(x)
        return jnp.concatenate([high, low, high], axis=0)

    for k in range(8):
        f_ref[k] = block_of(force_ref, k, 0)
    copies[0].wait()
    for k in range(8):
        put_end(k, f_ref[k])
    copies[1].wait()
    initial = jnp.concatenate([lg_ref[0, 0, 0:32], lg_ref[0, 0, 64:96]], axis=1)
    hom = dot(pc_ref[:, :, 768:832].reshape(512, 64), twice(initial))
    carry = coarse() + hom
    hom_ref[0] = carry_ref[0] = triple(initial.astype(f32))
    for k in range(7):
        hom_ref[k + 1] = triple(rows_of(hom, k))
        carry_ref[k + 1] = triple(rows_of(carry, k))
    factor = couplings(coupling_ref[...], 2)

    def piece(k, u):
        n, row = 4 * k + u, u * 64

        rows = jnp.concatenate(
            [p_ref[k, pl.ds(row, 64), 0:608], p_ref[k, pl.ds(row + 256, 64), 0:608]], axis=0
        )
        source = jnp.concatenate([f_ref[k], f_ref[k], carry_ref[k]], axis=0)
        real, imag = parts(dot(rows, source))
        j_at, h_at = 2 * k + u // 2, u % 2
        g = lg_ref[j_at, h_at, 128:256].astype(f32)
        spectral_re, spectral_im = spectral(real, imag, g[:64], g[64:], factor)
        s = jnp.concatenate([spectral_re, spectral_im], axis=1).astype(bf16)
        s_ref[k, pl.ds(row, 64)] = s
        y_ref[j_at, h_at, 0:64] = real.astype(bf16)
        y_ref[j_at, h_at, 64:128] = imag.astype(bf16)
        x_ref[n, 0:64], x_ref[n, 64:128] = real, imag

    def block(k, _):
        fetch(k).wait()
        for u in range(4):
            piece(k, u)
        return 0

    lax.fori_loop(0, 8, block, 0)
    for k in range(8):
        put_end(k, s_ref[k])
    carry = coarse()
    carry_ref[0] = jnp.zeros((96, 256), bf16)
    for k in range(7):
        carry_ref[k + 1] = triple(rows_of(carry, k))

    def own(ref):
        return jnp.concatenate(
            [ref[own_block, pl.ds(own_start, 64)], ref[own_block, pl.ds(own_low, 64)]], axis=0
        )

    p_own, s_own = own(p_ref), s_ref[own_block]
    source = jnp.concatenate([s_own, s_own, carry_ref[own_block]], axis=0)
    real, imag = parts(dot(p_own[:, 0:608], source))
    t_ref[0:64], t_ref[64:128] = real.astype(bf16), imag.astype(bf16)
    real, imag = parts(dot(p_own[:, 512:608], hom_ref[own_block]))
    base = x_ref[2 * j + h]
    base_ref[0:64] = 0.5 * (base[0:64] + real)
    base_ref[64:128] = 0.5 * (base[64:128] + imag)


PRED_SCRATCH = [
    pltpu.VMEM((8, 512, 640), bf16),
    pltpu.VMEM((8, 64, 512), bf16),
    pltpu.VMEM((8, 64, 896), bf16),
    pltpu.VMEM((8, 256, 256), bf16),
    pltpu.VMEM((8, 256, 256), bf16),
    pltpu.VMEM((3, 8, 32, 256), bf16),
    pltpu.VMEM((8, 96, 256), bf16),
    pltpu.VMEM((8, 96, 256), bf16),
    pltpu.VMEM((32, 128, 128), f32),
    pltpu.SemaphoreType.DMA((10,)),
]
FIRST_SCRATCH = [pltpu.VMEM((256, 256), f32)]


def call(kernel, outs, scratch, ins, flops, moved, grant=24, place=VMEM):
    return pl.pallas_call(
        kernel,
        out_shape=outs,
        in_specs=ins,
        out_specs=jax.tree.map(lambda _: place, outs),
        scratch_shapes=scratch,
        compiler_params=pltpu.CompilerParams(vmem_limit_bytes=int(grant * (1 << 20))),
        cost_estimate=pl.CostEstimate(flops=flops, bytes_accessed=moved, transcendentals=0),
    )


def shape(*dims, kind=bf16):
    return jax.ShapeDtypeStruct(dims, kind)


def shards(window, damping, propagator, coupling):
    orbitals = coupling.shape[0]
    horizon = damping.shape[0] * lax.axis_size(FIRST)
    scale = 1.0 / (horizon * math.sqrt(orbitals))
    where = jnp.stack([lax.axis_index(axis) for axis in (PLANE, "zh", "c")]).astype(jnp.int32)

    strength = coupling.reshape(1, 32)
    message = call(
        compose,
        shape(400, 128),
        [],
        [VMEM, VMEM, VMEM],
        40 * 64 * 128,
        400 << 10,
        63.9,
    )(window.reshape(2, 2, 64, 128), damping, strength)
    pair = lax.all_gather(message, "zh")
    lg = from_everyone(pair[:, :272], PLANE)

    s_rows = lax.all_gather(pair[:, 272:], "zm")
    s_rows = lax.all_gather(s_rows, "zq")
    s_other = swapped(s_rows, "c")

    c1 = call(
        functools.partial(first_collision, scale),
        shape(16, 2, 128, 128),
        FIRST_SCRATCH,
        [SMEM, VMEM, VMEM, VMEM],
        2 * 256 * 256 * 2048,
        4 << 20,
    )(where, s_rows, s_other, lg)
    force = lax.all_to_all(c1, PLANE, 0, 0, tiled=True)

    parts = lg[:, :, 256:258].reshape(64, 128).astype(f32)
    damp = parts[:, 0:32] + (parts[:, 32:64] + parts[:, 64:96])
    damp = jnp.tile(damp.T, (2, 1))
    plan = call(
        build_steps,
        shape(8, 640, 1024),
        [
            pltpu.VMEM((8, 512, 640), bf16),
            pltpu.VMEM((8, 64, 512), bf16),
            pltpu.VMEM((8, 64, 896), bf16),
            pltpu.VMEM((8, 64, 256), f32),
            pltpu.SemaphoreType.DMA((10,)),
        ],
        [VMEM, VMEM],
        64 * 2 * 64 * 256 * 256,
        6 << 20,
        54,
        HBM,
    )(damp, propagator.reshape(64, 32))

    y2, t2, base = call(
        predict,
        (shape(16, 2, 128, 128), shape(128, 128), shape(128, 128, kind=f32)),
        PRED_SCRATCH,
        [SMEM] + [VMEM] * 3 + [HBM],
        2 * 8 * 512 * 512 * 128 * 2,
        10 << 20,
        44,
    )(where, force, lg, strength, plan)

    t_rows = from_everyone(lax.all_gather(t2, "zm"), "zq")
    t_other = swapped(t_rows, "c")
    out = call(
        functools.partial(last_collision, scale),
        shape(2, 64, 128, kind=f32),
        [pltpu.VMEM((128, 256), f32)],
        [SMEM, VMEM, VMEM, VMEM, VMEM],
        2 * 128 * 256 * 2048,
        2 << 20,
    )(where, t_rows, t_other, y2, base)
    return out.reshape(2, 2, orbitals, 128)


def solution(mesh):
    finer = Mesh(mesh.devices.reshape(4, 4, 2, 2, 4, 2), (*FIRST, *SECOND))
    placed = (P(None, None, FIRST, None, SECOND), P(FIRST, None), P(), P())
    return jax.shard_map(
        shards, mesh=finer, in_specs=placed, out_specs=P(None, FIRST, None, SECOND), check_vma=False
    )
```

```python
import functools
import math

import jax
import jax.numpy as jnp
from jax import lax
from jax.experimental import pallas as pl
from jax.experimental.pallas import tpu as pltpu
from jax.sharding import Mesh
from jax.sharding import PartitionSpec as P

FIRST = ("y", "x", "zh")
SECOND = ("zm", "zq", "c")
PLANE = ("y", "x")
f32, bf16 = jnp.float32, jnp.bfloat16
VMEM = pl.BlockSpec(memory_space=pltpu.VMEM)
SMEM = pl.BlockSpec(memory_space=pltpu.SMEM)
HBM = pl.BlockSpec(memory_space=pltpu.HBM)


def from_everyone(shard, axis):
    peers = lax.axis_size(axis)
    return lax.all_to_all(
        jnp.broadcast_to(shard[None], (peers, *shard.shape)), axis, 0, 0, tiled=True
    )


def swapped(shard, axis):
    return lax.ppermute(shard, axis, [(0, 1), (1, 0)])


def couplings(row, times):
    wide = jnp.broadcast_to(row, (32, 32))
    at_row = lax.broadcasted_iota(jnp.int32, (32, 32), 0)
    at_lane = lax.broadcasted_iota(jnp.int32, (32, 32), 1)
    column = jnp.sum(jnp.where(at_row == at_lane, wide, 0.0), axis=1, keepdims=True)
    tile = jnp.concatenate([column * wide] * 4, axis=1)
    return jnp.concatenate([tile] * times, axis=0)


def spectral(less_re, less_im, great_re, great_im, factor):
    lsquare_re = less_re * less_re - less_im * less_im
    lsquare_im = 2.0 * less_re * less_im
    gsquare_re = great_re * great_re - great_im * great_im
    gsquare_im = 2.0 * great_re * great_im
    real = (lsquare_re * great_re + lsquare_im * great_im) - (
        gsquare_re * less_re + gsquare_im * less_im
    )
    imag = (lsquare_im * great_re - lsquare_re * great_im) - (
        gsquare_im * less_re - gsquare_re * less_im
    )
    return factor * real, factor * imag


def dot(left, right):
    return jnp.dot(left, right, preferred_element_type=f32)


def compose(window_ref, damp_ref, coupling_ref, out_ref):
    fields = [[window_ref[which, part] for part in range(2)] for which in range(2)]
    for which in range(2):
        for part in range(2):
            start = 128 * which + 64 * part
            out_ref[start : start + 64] = fields[which][part].astype(bf16)
    damp = damp_ref[...]
    high = damp.astype(bf16).astype(f32)
    mid = (damp - high).astype(bf16).astype(f32)
    low = damp - high - mid
    rows = jnp.concatenate([high, mid, low, jnp.zeros_like(low)], axis=1)
    out_ref[256:272] = jnp.concatenate([rows, jnp.zeros((14, 128), f32)], axis=0).astype(bf16)
    real, imag = spectral(*fields[0], *fields[1], couplings(coupling_ref[...], 2))
    out_ref[272:336], out_ref[336:400] = real.astype(bf16), imag.astype(bf16)


def compose(window_ref, damp_ref, coupling_ref, out_ref):
    fields = [[window_ref[which, part] for part in range(2)] for which in range(2)]
    for which in range(2):
        for part in range(2):
            start = 128 * which + 64 * part
            out_ref[start : start + 64] = fields[which][part].astype(bf16)
    damp = damp_ref[...]
    high = damp.astype(bf16).astype(f32)
    mid = (damp - high).astype(bf16).astype(f32)
    low = damp - high - mid
    rows = jnp.concatenate([high, mid, low, jnp.zeros_like(low)], axis=1)
    out_ref[256:272] = jnp.concatenate([rows, jnp.zeros((14, 128), f32)], axis=0).astype(bf16)
    real, imag = spectral(*fields[0], *fields[1], couplings(coupling_ref[...], 2))
    out_ref[272:336], out_ref[336:400] = real.astype(bf16), imag.astype(bf16)


def row_times_column(pieces, y_ref, acc_ref):
    for n, (left, blocks) in enumerate(pieces):
        right = [
            jnp.concatenate(
                [y_ref[j, :, 0:64].reshape(128, 128), y_ref[j, :, 64:128].reshape(128, 128)],
                axis=1,
            )
            for j in blocks
        ]
        part = dot(jnp.concatenate(left, axis=1), jnp.concatenate(right, axis=0))
        if n == 0:
            acc_ref[...] = part
        else:
            acc_ref[...] += part


def half_product(side, s_ref, y_ref, acc_ref):
    for q in range(4):
        left = jnp.concatenate([s_ref[q, m].reshape(-1, 128) for m in range(2)], axis=1)
        right = []
        for m in range(2):
            j = 8 * m + 2 * q + side
            right.append(
                jnp.concatenate(
                    [y_ref[j, :, 0:64].reshape(128, 128), y_ref[j, :, 64:128].reshape(128, 128)],
                    axis=1,
                )
            )
        part = dot(left, jnp.concatenate(right, axis=0))
        if q == 0:
            acc_ref[...] = part
        else:
            acc_ref[...] += part


def own_half(where_ref, s_ref, y_ref, acc_ref):
    half_product(where_ref[2], s_ref, y_ref, acc_ref)


def first_collision(scale, where_ref, s_ref, y_ref, own_ref, out_ref, acc_ref):
    half_product(1 - where_ref[2], s_ref, y_ref, acc_ref)
    acc_ref[...] += own_ref[...]
    for h in range(2):
        top, low = acc_ref[h * 128 : h * 128 + 64], acc_ref[h * 128 + 64 : h * 128 + 128]
        real = (scale * (top[:, :128] - low[:, 128:])).astype(bf16)
        imag = (scale * (top[:, 128:] + low[:, :128])).astype(bf16)
        out_ref[h, 0:64], out_ref[h, 64:128] = real, imag


def last_collision(scale, where_ref, s_ref, y_ref, own_ref, base_ref, out_ref, acc_ref):
    half_product(1 - where_ref[2], s_ref, y_ref, acc_ref)
    acc_ref[...] += own_ref[...]
    top, low = acc_ref[0:64], acc_ref[64:128]
    out_ref[0] = base_ref[0:64] + (0.5 * scale) * (top[:, :128] - low[:, 128:])
    out_ref[1] = base_ref[64:128] + (0.5 * scale) * (top[:, 128:] + low[:, :128])


def halves(x):
    high = x.astype(bf16)
    return high, (x - high.astype(f32)).astype(bf16)


def long_product(left, right):
    lh, ll = left
    rh, rl = halves(right)
    return dot(
        jnp.concatenate([lh, lh, ll, ll], axis=1), jnp.concatenate([rh, rl, rh, rl], axis=0)
    )


def embedded(z):
    return jnp.concatenate([z, jnp.concatenate([-z[32:], z[:32]], axis=0)], axis=1)


def put_unit(z, at):
    row = lax.broadcasted_iota(jnp.int32, z.shape, 0)
    lane = lax.broadcasted_iota(jnp.int32, z.shape, 1)
    unit = jnp.where((row == lane - 32 * at) & (row < 32), 1.0, 0.0)
    return jnp.where(lane >= 32 * at, unit, z)


def lanes_from_zero(z, last):
    moved = jnp.concatenate([z[:, 32:], z[:, :32]], axis=1)
    row = lax.broadcasted_iota(jnp.int32, z.shape, 0)
    lane = lax.broadcasted_iota(jnp.int32, z.shape, 1)
    tail = jnp.where(row == lane - 224, 1.0, 0.0) if last else jnp.zeros_like(z)
    return jnp.where(lane >= 224, tail, moved)


def build_steps(damp_ref, u_ref, out_hbm, p_ref, last_ref, pc_ref, z_ref, sems):
    copies = [
        pltpu.make_async_copy(p_ref.at[k], out_hbm.at[k, 0:512, 0:640], sems.at[k])
        for k in range(8)
    ]
    copies.append(pltpu.make_async_copy(last_ref, out_hbm.at[:, 512:640, 0:256], sems.at[8]))
    copies.append(pltpu.make_async_copy(pc_ref, out_hbm.at[:, 640:704, 0:896], sems.at[9]))
    left = halves(embedded(u_ref[...]))

    def store(k, i, z):
        high, low = halves(lanes_from_zero(z, i == 7))
        first_high, first_low = halves(z[:, :32])
        first = jnp.concatenate([first_high, first_high, first_low], axis=1)
        for part in range(2):
            start = 256 * part + 32 * i
            rows, to = slice(32 * part, 32 * part + 32), slice(start, start + 32)
            p_ref[k, to, 0:256] = high[rows]
            p_ref[k, to, 256:512] = low[rows]
            p_ref[k, to, 512:608] = first[rows]
            if i == 7:
                last_ref[k, rows] = high[rows]
                last_ref[k, 64 + 32 * part : 96 + 32 * part] = low[rows]

    for k in range(8):
        start = jnp.concatenate([u_ref[...], jnp.zeros((64, 224), f32)], axis=1)
        z = put_unit(damp_ref[:, 8 * k : 8 * k + 1] * start, 1)
        z_ref[k] = z
        store(k, 0, z)
    for i in range(1, 8):
        for k in range(8):
            t = 8 * k + i
            z = damp_ref[:, t : t + 1] * long_product(left, z_ref[k])
            if i < 7:
                z = put_unit(z, i + 1)
            z_ref[k] = z
            store(k, i, z)
            if i == 7:
                copies[k].start()
    copies[8].start()

    w = None
    for k in range(8):
        whole = z_ref[k][:, :32]
        if k == 0:
            w = put_unit(jnp.concatenate([whole, jnp.zeros((64, 224), f32)], axis=1), 1)
        else:
            w = long_product(halves(embedded(whole)), w)
            if k < 7:
                w = put_unit(w, k + 1)
        high, low = halves(lanes_from_zero(w, k == 7))
        pc_ref[k, :, 0:256] = high
        pc_ref[k, :, 256:512] = high
        pc_ref[k, :, 512:768] = low
        pc_ref[k, :, 768:832] = jnp.concatenate(halves(w[:, :32]), axis=1)
    copies[9].start()
    for copy in copies:
        copy.wait()


def predict(
    where_ref, force_ref, lg_ref, coupling_ref, plan_hbm,
    y_ref, t_ref, base_ref,
    p_ref, last_ref, pc_ref, f_ref, s_ref, ends_ref, carry_ref, hom_ref, x_ref, sems,
):
    copies = [
        pltpu.make_async_copy(plan_hbm.at[:, 512:640, 0:256], last_ref, sems.at[8]),
        pltpu.make_async_copy(plan_hbm.at[:, 640:704, 0:896], pc_ref, sems.at[9]),
    ]

    def fetch(k):
        return pltpu.make_async_copy(
            plan_hbm.at[k, 0:512, 0:640], p_ref.at[k], sems.at[k]
        )

    for copy in copies + [fetch(k) for k in range(8)]:
        copy.start()

    j, h = where_ref[0], where_ref[1]
    own_block, own_start = j // 2, pl.multiple_of((j % 2) * 128 + h * 64, 64)
    own_low = pl.multiple_of(own_start + 256, 64)

    def block_of(ref, k, start):
        return jnp.concatenate(
            [
                jnp.concatenate(
                    [
                        ref[2 * k + u // 2, u % 2, start + 64 * part : start + 64 * part + 64]
                        for u in range(4)
                    ],
                    axis=0,
                )
                for part in range(2)
            ],
            axis=1,
        )

    def parts(product):
        rows = product.shape[0] // 2
        top, low = product[:rows], product[rows:]
        return top[:, :128] - low[:, 128:], top[:, 128:] + low[:, :128]

    def twice(x):
        return jnp.concatenate([x, x], axis=0)

    def put_end(k, source):
        product = dot(last_ref[k], source)
        real, imag = parts(product[:64] + product[64:])
        high, low = halves(jnp.concatenate([real, imag], axis=1))
        ends_ref[0, k], ends_ref[1, k], ends_ref[2, k] = high, low, high

    def coarse():
        return dot(pc_ref[:, :, 0:768].reshape(512, 768), ends_ref[...].reshape(768, 256))

    def rows_of(product, k):
        part = product[k * 64 : k * 64 + 64]
        return jnp.concatenate(parts(part), axis=1)

    def triple(x):
        high, low = halves(x)
        return jnp.concatenate([high, low, high], axis=0)

    for k in range(8):
        f_ref[k] = block_of(force_ref, k, 0)
    copies[0].wait()
    for k in range(8):
        put_end(k, f_ref[k])
    copies[1].wait()
    initial = jnp.concatenate([lg_ref[0, 0, 0:32], lg_ref[0, 0, 64:96]], axis=1)
    hom = dot(pc_ref[:, :, 768:832].reshape(512, 64), twice(initial))
    carry = coarse() + hom
    hom_ref[0] = carry_ref[0] = triple(initial.astype(f32))
    for k in range(7):
        hom_ref[k + 1] = triple(rows_of(hom, k))
        carry_ref[k + 1] = triple(rows_of(carry, k))
    factor = couplings(coupling_ref[...], 2)

    def piece(k, u):
        n, row = 4 * k + u, u * 64

        rows = jnp.concatenate(
            [p_ref[k, pl.ds(row, 64), 0:608], p_ref[k, pl.ds(row + 256, 64), 0:608]], axis=0
        )
        source = jnp.concatenate([f_ref[k], f_ref[k], carry_ref[k]], axis=0)
        real, imag = parts(dot(rows, source))
        j_at, h_at = 2 * k + u // 2, u % 2
        g = lg_ref[j_at, h_at, 128:256].astype(f32)
        spectral_re, spectral_im = spectral(real, imag, g[:64], g[64:], factor)
        s = jnp.concatenate([spectral_re, spectral_im], axis=1).astype(bf16)
        s_ref[k, pl.ds(row, 64)] = s
        y_ref[j_at, h_at, 0:64] = real.astype(bf16)
        y_ref[j_at, h_at, 64:128] = imag.astype(bf16)
        x_ref[n, 0:64], x_ref[n, 64:128] = real, imag

    def block(k, _):
        fetch(k).wait()
        for u in range(4):
            piece(k, u)
        return 0

    lax.fori_loop(0, 8, block, 0)
    for k in range(8):
        put_end(k, s_ref[k])
    carry = coarse()
    carry_ref[0] = jnp.zeros((96, 256), bf16)
    for k in range(7):
        carry_ref[k + 1] = triple(rows_of(carry, k))

    def own(ref):
        return jnp.concatenate(
            [ref[own_block, pl.ds(own_start, 64)], ref[own_block, pl.ds(own_low, 64)]], axis=0
        )

    p_own, s_own = own(p_ref), s_ref[own_block]
    source = jnp.concatenate([s_own, s_own, carry_ref[own_block]], axis=0)
    real, imag = parts(dot(p_own[:, 0:608], source))
    t_ref[0:64], t_ref[64:128] = real.astype(bf16), imag.astype(bf16)
    real, imag = parts(dot(p_own[:, 512:608], hom_ref[own_block]))
    base = x_ref[2 * j + h]
    base_ref[0:64] = 0.5 * (base[0:64] + real)
    base_ref[64:128] = 0.5 * (base[64:128] + imag)


PRED_SCRATCH = [
    pltpu.VMEM((8, 512, 640), bf16),
    pltpu.VMEM((8, 128, 256), bf16),
    pltpu.VMEM((8, 64, 896), bf16),
    pltpu.VMEM((8, 256, 256), bf16),
    pltpu.VMEM((8, 256, 256), bf16),
    pltpu.VMEM((3, 8, 32, 256), bf16),
    pltpu.VMEM((8, 96, 256), bf16),
    pltpu.VMEM((8, 96, 256), bf16),
    pltpu.VMEM((32, 128, 128), f32),
    pltpu.SemaphoreType.DMA((10,)),
]


def call(kernel, outs, scratch, ins, flops, moved, grant=24, place=VMEM):
    return pl.pallas_call(
        kernel,
        out_shape=outs,
        in_specs=ins,
        out_specs=jax.tree.map(lambda _: place, outs),
        scratch_shapes=scratch,
        compiler_params=pltpu.CompilerParams(vmem_limit_bytes=int(grant * (1 << 20))),
        cost_estimate=pl.CostEstimate(flops=flops, bytes_accessed=moved, transcendentals=0),
    )


def shape(*dims, kind=bf16):
    return jax.ShapeDtypeStruct(dims, kind)


def shards(window, damping, propagator, coupling):
    orbitals = coupling.shape[0]
    horizon = damping.shape[0] * lax.axis_size(FIRST)
    scale = 1.0 / (horizon * math.sqrt(orbitals))
    where = jnp.stack([lax.axis_index(axis) for axis in (PLANE, "zh", "c")]).astype(jnp.int32)

    strength = coupling.reshape(1, 32)
    message = call(
        compose,
        shape(400, 128),
        [],
        [VMEM, VMEM, VMEM],
        40 * 64 * 128,
        400 << 10,
        63.9,
    )(window.reshape(2, 2, 64, 128), damping, strength)
    pair = lax.all_gather(message, "zh")
    lg = from_everyone(pair[:, :272], PLANE)

    s_rows = lax.all_gather(pair[:, 272:], "zm")
    s_rows = lax.all_gather(s_rows, "zq")
    s_other = swapped(s_rows, "c")

    own = call(
        own_half,
        shape(256, 256, kind=f32),
        [],
        [SMEM, VMEM, VMEM],
        256 * 256 * 2048,
        2 << 20,
    )(where, s_rows, lg)
    c1 = call(
        functools.partial(first_collision, scale),
        shape(2, 128, 128),
        [pltpu.VMEM((256, 256), f32)],
        [SMEM, VMEM, VMEM, VMEM],
        256 * 256 * 2048,
        3 << 20,
    )(where, s_other, lg, own)
    force = from_everyone(c1, PLANE)

    parts = lg[:, :, 256:258].reshape(64, 128).astype(f32)
    damp = parts[:, 0:32] + (parts[:, 32:64] + parts[:, 64:96])
    damp = jnp.tile(damp.T, (2, 1))
    plan = call(
        build_steps,
        shape(8, 704, 1024),
        [
            pltpu.VMEM((8, 512, 640), bf16),
            pltpu.VMEM((8, 128, 256), bf16),
            pltpu.VMEM((8, 64, 896), bf16),
            pltpu.VMEM((8, 64, 256), f32),
            pltpu.SemaphoreType.DMA((10,)),
        ],
        [VMEM, VMEM],
        64 * 2 * 64 * 256 * 256,
        6 << 20,
        54,
        HBM,
    )(damp, propagator.reshape(64, 32))

    y2, t2, base = call(
        predict,
        (shape(16, 2, 128, 128), shape(128, 128), shape(128, 128, kind=f32)),
        PRED_SCRATCH,
        [SMEM] + [VMEM] * 3 + [HBM],
        2 * 8 * 512 * 512 * 128 * 2,
        10 << 20,
        44,
    )(where, force, lg, strength, plan)

    t_rows = from_everyone(lax.all_gather(t2, "zm"), "zq")
    t_other = swapped(t_rows, "c")
    own = call(
        own_half,
        shape(128, 256, kind=f32),
        [],
        [SMEM, VMEM, VMEM],
        128 * 256 * 2048,
        1 << 20,
    )(where, t_rows, y2)
    out = call(
        functools.partial(last_collision, scale),
        shape(2, 64, 128, kind=f32),
        [pltpu.VMEM((128, 256), f32)],
        [SMEM, VMEM, VMEM, VMEM, VMEM],
        128 * 256 * 2048,
        1 << 20,
    )(where, t_other, y2, own, base)
    return out.reshape(2, 2, orbitals, 128)


def solution(mesh):
    finer = Mesh(mesh.devices.reshape(4, 4, 2, 2, 4, 2), (*FIRST, *SECOND))
    placed = (P(None, None, FIRST, None, SECOND), P(FIRST, None), P(), P())
    return jax.shard_map(
        shards, mesh=finer, in_specs=placed, out_specs=P(None, FIRST, None, SECOND), check_vma=False
    )
```

```python
import functools
import math

import jax
import jax.numpy as jnp
from jax import lax
from jax.experimental import pallas as pl
from jax.experimental.pallas import tpu as pltpu
from jax.sharding import Mesh
from jax.sharding import PartitionSpec as P

FIRST = ("y", "x", "zh")
SECOND = ("zm", "zq", "c")
PLANE = ("y", "x")
f32, bf16 = jnp.float32, jnp.bfloat16
VMEM = pl.BlockSpec(memory_space=pltpu.VMEM)
SMEM = pl.BlockSpec(memory_space=pltpu.SMEM)
HBM = pl.BlockSpec(memory_space=pltpu.HBM)


def from_everyone(shard, axis):
    peers = lax.axis_size(axis)
    return lax.all_to_all(
        jnp.broadcast_to(shard[None], (peers, *shard.shape)), axis, 0, 0, tiled=True
    )


def swapped(shard, axis):
    return lax.ppermute(shard, axis, [(0, 1), (1, 0)])


def couplings(row, times):
    wide = jnp.broadcast_to(row, (32, 32))
    at_row = lax.broadcasted_iota(jnp.int32, (32, 32), 0)
    at_lane = lax.broadcasted_iota(jnp.int32, (32, 32), 1)
    column = jnp.sum(jnp.where(at_row == at_lane, wide, 0.0), axis=1, keepdims=True)
    tile = jnp.concatenate([column * wide] * 4, axis=1)
    return jnp.concatenate([tile] * times, axis=0)


def spectral(less_re, less_im, great_re, great_im, factor):
    lsquare_re = less_re * less_re - less_im * less_im
    lsquare_im = 2.0 * less_re * less_im
    gsquare_re = great_re * great_re - great_im * great_im
    gsquare_im = 2.0 * great_re * great_im
    real = (lsquare_re * great_re + lsquare_im * great_im) - (
        gsquare_re * less_re + gsquare_im * less_im
    )
    imag = (lsquare_im * great_re - lsquare_re * great_im) - (
        gsquare_im * less_re - gsquare_re * less_im
    )
    return factor * real, factor * imag


def dot(left, right):
    return jnp.dot(left, right, preferred_element_type=f32)


def compose(window_ref, damp_ref, coupling_ref, out_ref):
    fields = [[window_ref[which, part] for part in range(2)] for which in range(2)]
    for which in range(2):
        for part in range(2):
            start = 128 * which + 64 * part
            out_ref[start : start + 64] = fields[which][part].astype(bf16)
    damp = damp_ref[...]
    high = damp.astype(bf16).astype(f32)
    mid = (damp - high).astype(bf16).astype(f32)
    low = damp - high - mid
    rows = jnp.concatenate([high, mid, low, jnp.zeros_like(low)], axis=1)
    out_ref[256:264] = jnp.concatenate([rows, jnp.zeros((6, 128), f32)], axis=0).astype(bf16)
    real, imag = spectral(*fields[0], *fields[1], couplings(coupling_ref[...], 2))
    out_ref[264:328], out_ref[328:392] = real.astype(bf16), imag.astype(bf16)


def row_times_column(pieces, y_ref, acc_ref):
    for n, (left, blocks) in enumerate(pieces):
        right = [
            jnp.concatenate(
                [y_ref[j, :, 0:64].reshape(128, 128), y_ref[j, :, 64:128].reshape(128, 128)],
                axis=1,
            )
            for j in blocks
        ]
        part = dot(jnp.concatenate(left, axis=1), jnp.concatenate(right, axis=0))
        if n == 0:
            acc_ref[...] = part
        else:
            acc_ref[...] += part


def first_collision(scale, where_ref, own_ref, other_ref, y_ref, out_ref, acc_ref):
    core = where_ref[2]
    pieces = [
        (
            [s_ref[q, m].reshape(256, 128) for m in range(2)],
            [8 * m + 2 * q + side for m in range(2)],
        )
        for s_ref, side in ((own_ref, core), (other_ref, 1 - core))
        for q in range(4)
    ]
    row_times_column(pieces, y_ref, acc_ref)
    for h in range(2):
        top, low = acc_ref[h * 128 : h * 128 + 64], acc_ref[h * 128 + 64 : h * 128 + 128]
        real = (scale * (top[:, :128] - low[:, 128:])).astype(bf16)
        imag = (scale * (top[:, 128:] + low[:, :128])).astype(bf16)
        for peer in range(16):
            out_ref[peer, h, 0:64] = real
            out_ref[peer, h, 64:128] = imag


def last_collision(scale, where_ref, own_ref, other_ref, y_ref, base_ref, out_ref, acc_ref):
    core = where_ref[2]
    pieces = [
        ([s_ref[q, m] for m in range(2)], [8 * m + 2 * q + side for m in range(2)])
        for s_ref, side in ((own_ref, core), (other_ref, 1 - core))
        for q in range(4)
    ]
    row_times_column(pieces, y_ref, acc_ref)
    top, low = acc_ref[0:64], acc_ref[64:128]
    out_ref[0] = base_ref[0:64] + (0.5 * scale) * (top[:, :128] - low[:, 128:])
    out_ref[1] = base_ref[64:128] + (0.5 * scale) * (top[:, 128:] + low[:, :128])


def halves(x):
    high = x.astype(bf16)
    return high, (x - high.astype(f32)).astype(bf16)


def long_product(left, right):
    lh, ll = left
    rh, rl = halves(right)
    return dot(
        jnp.concatenate([lh, lh, ll, ll], axis=1), jnp.concatenate([rh, rl, rh, rl], axis=0)
    )


def embedded(z):
    return jnp.concatenate([z, jnp.concatenate([-z[32:], z[:32]], axis=0)], axis=1)


def put_unit(z, at):
    row = lax.broadcasted_iota(jnp.int32, z.shape, 0)
    lane = lax.broadcasted_iota(jnp.int32, z.shape, 1)
    unit = jnp.where((row == lane - 32 * at) & (row < 32), 1.0, 0.0)
    return jnp.where(lane >= 32 * at, unit, z)


def lanes_from_zero(z, last):
    moved = jnp.concatenate([z[:, 32:], z[:, :32]], axis=1)
    row = lax.broadcasted_iota(jnp.int32, z.shape, 0)
    lane = lax.broadcasted_iota(jnp.int32, z.shape, 1)
    tail = jnp.where(row == lane - 224, 1.0, 0.0) if last else jnp.zeros_like(z)
    return jnp.where(lane >= 224, tail, moved)


def build_steps(damp_ref, u_ref, out_hbm, p_ref, last_ref, pc_ref, z_ref, sems):
    copies = [
        pltpu.make_async_copy(p_ref.at[k], out_hbm.at[k, 0:512, 0:640], sems.at[k])
        for k in range(8)
    ]
    copies.append(pltpu.make_async_copy(last_ref, out_hbm.at[:, 512:640, 0:256], sems.at[8]))
    copies.append(pltpu.make_async_copy(pc_ref, out_hbm.at[:, 640:704, 0:896], sems.at[9]))
    left = halves(embedded(u_ref[...]))

    def store(k, i, z):
        high, low = halves(lanes_from_zero(z, i == 7))
        first_high, first_low = halves(z[:, :32])
        first = jnp.concatenate([first_high, first_high, first_low], axis=1)
        for part in range(2):
            start = 256 * part + 32 * i
            rows, to = slice(32 * part, 32 * part + 32), slice(start, start + 32)
            p_ref[k, to, 0:256] = high[rows]
            p_ref[k, to, 256:512] = low[rows]
            p_ref[k, to, 512:608] = first[rows]
            if i == 7:
                last_ref[k, rows] = high[rows]
                last_ref[k, 64 + 32 * part : 96 + 32 * part] = low[rows]

    for k in range(8):
        start = jnp.concatenate([u_ref[...], jnp.zeros((64, 224), f32)], axis=1)
        z = put_unit(damp_ref[:, 8 * k : 8 * k + 1] * start, 1)
        z_ref[k] = z
        store(k, 0, z)
    for i in range(1, 8):
        for k in range(8):
            t = 8 * k + i
            z = damp_ref[:, t : t + 1] * long_product(left, z_ref[k])
            if i < 7:
                z = put_unit(z, i + 1)
            z_ref[k] = z
            store(k, i, z)
            if i == 7:
                copies[k].start()
    copies[8].start()

    w = None
    for k in range(8):
        whole = z_ref[k][:, :32]
        if k == 0:
            w = put_unit(jnp.concatenate([whole, jnp.zeros((64, 224), f32)], axis=1), 1)
        else:
            w = long_product(halves(embedded(whole)), w)
            if k < 7:
                w = put_unit(w, k + 1)
        high, low = halves(lanes_from_zero(w, k == 7))
        pc_ref[k, :, 0:256] = high
        pc_ref[k, :, 256:512] = high
        pc_ref[k, :, 512:768] = low
        pc_ref[k, :, 768:832] = jnp.concatenate(halves(w[:, :32]), axis=1)
    copies[9].start()
    for copy in copies:
        copy.wait()


def predict(
    where_ref, force_ref, lg_ref, coupling_ref, plan_hbm,
    y_ref, t_ref, base_ref,
    p_ref, last_ref, pc_ref, f_ref, s_ref, ends_ref, carry_ref, hom_ref, x_ref, sems,
):
    copies = [
        pltpu.make_async_copy(plan_hbm.at[:, 512:640, 0:256], last_ref, sems.at[8]),
        pltpu.make_async_copy(plan_hbm.at[:, 640:704, 0:896], pc_ref, sems.at[9]),
    ]

    def fetch(k):
        return pltpu.make_async_copy(
            plan_hbm.at[k, 0:512, 0:640], p_ref.at[k], sems.at[k]
        )

    for copy in copies + [fetch(k) for k in range(8)]:
        copy.start()

    j, h = where_ref[0], where_ref[1]
    own_block, own_start = j // 2, pl.multiple_of((j % 2) * 128 + h * 64, 64)
    own_low = pl.multiple_of(own_start + 256, 64)

    def block_of(ref, k, start):
        return jnp.concatenate(
            [
                jnp.concatenate(
                    [
                        ref[2 * k + u // 2, u % 2, start + 64 * part : start + 64 * part + 64]
                        for u in range(4)
                    ],
                    axis=0,
                )
                for part in range(2)
            ],
            axis=1,
        )

    def parts(product):
        rows = product.shape[0] // 2
        top, low = product[:rows], product[rows:]
        return top[:, :128] - low[:, 128:], top[:, 128:] + low[:, :128]

    def twice(x):
        return jnp.concatenate([x, x], axis=0)

    def put_end(k, source):
        product = dot(last_ref[k], source)
        real, imag = parts(product[:64] + product[64:])
        high, low = halves(jnp.concatenate([real, imag], axis=1))
        ends_ref[0, k], ends_ref[1, k], ends_ref[2, k] = high, low, high

    def coarse():
        return dot(pc_ref[:, :, 0:768].reshape(512, 768), ends_ref[...].reshape(768, 256))

    def rows_of(product, k):
        part = product[k * 64 : k * 64 + 64]
        return jnp.concatenate(parts(part), axis=1)

    def triple(x):
        high, low = halves(x)
        return jnp.concatenate([high, low, high], axis=0)

    for k in range(8):
        f_ref[k] = block_of(force_ref, k, 0)
    copies[0].wait()
    for k in range(8):
        put_end(k, f_ref[k])
    copies[1].wait()
    initial = jnp.concatenate([lg_ref[0, 0, 0:32], lg_ref[0, 0, 64:96]], axis=1)
    hom = dot(pc_ref[:, :, 768:832].reshape(512, 64), twice(initial))
    carry = coarse() + hom
    hom_ref[0] = carry_ref[0] = triple(initial.astype(f32))
    for k in range(7):
        hom_ref[k + 1] = triple(rows_of(hom, k))
        carry_ref[k + 1] = triple(rows_of(carry, k))
    factor = couplings(coupling_ref[...], 2)

    def piece(k, u):
        n, row = 4 * k + u, u * 64

        width = 128 if u < 2 else 256
        rows = jnp.concatenate(
            [
                jnp.concatenate(
                    [p_ref[k, at : at + 64, lane : lane + width] for lane in (0, 256)]
                    + [p_ref[k, at : at + 64, 512:608]],
                    axis=1,
                )
                for at in (row, row + 256)
            ],
            axis=0,
        )
        force = f_ref[k, 0:width]
        source = jnp.concatenate([force, force, carry_ref[k]], axis=0)
        real, imag = parts(dot(rows, source))
        j_at, h_at = 2 * k + u // 2, u % 2
        g = lg_ref[j_at, h_at, 128:256].astype(f32)
        spectral_re, spectral_im = spectral(real, imag, g[:64], g[64:], factor)
        s = jnp.concatenate([spectral_re, spectral_im], axis=1).astype(bf16)
        s_ref[k, pl.ds(row, 64)] = s
        y_ref[j_at, h_at, 0:64] = real.astype(bf16)
        y_ref[j_at, h_at, 64:128] = imag.astype(bf16)
        x_ref[n, 0:64], x_ref[n, 64:128] = real, imag

    def block(k, _):
        fetch(k).wait()
        for u in range(4):
            piece(k, u)
        return 0

    lax.fori_loop(0, 8, block, 0)
    for k in range(8):
        put_end(k, s_ref[k])
    carry = coarse()
    carry_ref[0] = jnp.zeros((96, 256), bf16)
    for k in range(7):
        carry_ref[k + 1] = triple(rows_of(carry, k))

    def own(ref):
        return jnp.concatenate(
            [ref[own_block, pl.ds(own_start, 64)], ref[own_block, pl.ds(own_low, 64)]], axis=0
        )

    p_own, s_own = own(p_ref), s_ref[own_block]
    source = jnp.concatenate([s_own, s_own, carry_ref[own_block]], axis=0)
    real, imag = parts(dot(p_own[:, 0:608], source))
    t_ref[0:64], t_ref[64:128] = real.astype(bf16), imag.astype(bf16)
    real, imag = parts(dot(p_own[:, 512:608], hom_ref[own_block]))
    base = x_ref[2 * j + h]
    base_ref[0:64] = 0.5 * (base[0:64] + real)
    base_ref[64:128] = 0.5 * (base[64:128] + imag)


PRED_SCRATCH = [
    pltpu.VMEM((8, 512, 640), bf16),
    pltpu.VMEM((8, 128, 256), bf16),
    pltpu.VMEM((8, 64, 896), bf16),
    pltpu.VMEM((8, 256, 256), bf16),
    pltpu.VMEM((8, 256, 256), bf16),
    pltpu.VMEM((3, 8, 32, 256), bf16),
    pltpu.VMEM((8, 96, 256), bf16),
    pltpu.VMEM((8, 96, 256), bf16),
    pltpu.VMEM((32, 128, 128), f32),
    pltpu.SemaphoreType.DMA((10,)),
]


def call(kernel, outs, scratch, ins, flops, moved, grant=24, place=VMEM):
    return pl.pallas_call(
        kernel,
        out_shape=outs,
        in_specs=ins,
        out_specs=jax.tree.map(lambda _: place, outs),
        scratch_shapes=scratch,
        compiler_params=pltpu.CompilerParams(vmem_limit_bytes=int(grant * (1 << 20))),
        cost_estimate=pl.CostEstimate(flops=flops, bytes_accessed=moved, transcendentals=0),
    )


def shape(*dims, kind=bf16):
    return jax.ShapeDtypeStruct(dims, kind)


def shards(window, damping, propagator, coupling):
    orbitals = coupling.shape[0]
    horizon = damping.shape[0] * lax.axis_size(FIRST)
    scale = 1.0 / (horizon * math.sqrt(orbitals))
    where = jnp.stack([lax.axis_index(axis) for axis in (PLANE, "zh", "c")]).astype(jnp.int32)

    strength = coupling.reshape(1, 32)
    message = call(
        compose,
        shape(392, 128),
        [],
        [VMEM, VMEM, VMEM],
        40 * 64 * 128,
        400 << 10,
        63.9,
    )(window.reshape(2, 2, 64, 128), damping, strength)
    pair = lax.all_gather(message, "zh")
    lg = from_everyone(pair[:, :264], PLANE)

    s_rows = lax.all_gather(pair[:, 264:], "zm")
    s_rows = lax.all_gather(s_rows, "zq")
    s_other = swapped(s_rows, "c")

    c1 = call(
        functools.partial(first_collision, scale),
        shape(16, 2, 128, 128),
        [pltpu.VMEM((256, 256), f32)],
        [SMEM, VMEM, VMEM, VMEM],
        2 * 256 * 256 * 2048,
        4 << 20,
    )(where, s_rows, s_other, lg)
    force = lax.all_to_all(c1, PLANE, 0, 0, tiled=True)

    parts = lg[:, :, 256:258].reshape(64, 128).astype(f32)
    damp = parts[:, 0:32] + (parts[:, 32:64] + parts[:, 64:96])
    damp = jnp.tile(damp.T, (2, 1))
    plan = call(
        build_steps,
        shape(8, 704, 1024),
        [
            pltpu.VMEM((8, 512, 640), bf16),
            pltpu.VMEM((8, 128, 256), bf16),
            pltpu.VMEM((8, 64, 896), bf16),
            pltpu.VMEM((8, 64, 256), f32),
            pltpu.SemaphoreType.DMA((10,)),
        ],
        [VMEM, VMEM],
        64 * 2 * 64 * 256 * 256,
        6 << 20,
        54,
        HBM,
    )(damp, propagator.reshape(64, 32))

    y2, t2, base = call(
        predict,
        (shape(16, 2, 128, 128), shape(128, 128), shape(128, 128, kind=f32)),
        PRED_SCRATCH,
        [SMEM] + [VMEM] * 3 + [HBM],
        2 * 8 * 512 * 512 * 128 * 2,
        10 << 20,
        44,
    )(where, force, lg, strength, plan)

    t_rows = from_everyone(lax.all_gather(t2, "zm"), "zq")
    t_other = swapped(t_rows, "c")
    out = call(
        functools.partial(last_collision, scale),
        shape(2, 64, 128, kind=f32),
        [pltpu.VMEM((128, 256), f32)],
        [SMEM, VMEM, VMEM, VMEM, VMEM],
        2 * 128 * 256 * 2048,
        2 << 20,
    )(where, t_rows, t_other, y2, base)
    return out.reshape(2, 2, orbitals, 128)


def solution(mesh):
    finer = Mesh(mesh.devices.reshape(4, 4, 2, 2, 4, 2), (*FIRST, *SECOND))
    placed = (P(None, None, FIRST, None, SECOND), P(FIRST, None), P(), P())
    return jax.shard_map(
        shards, mesh=finer, in_specs=placed, out_specs=P(None, FIRST, None, SECOND), check_vma=False
    )
```

```python
import functools
import math

import jax
import jax.numpy as jnp
from jax import lax
from jax.experimental import pallas as pl
from jax.experimental.pallas import tpu as pltpu
from jax.sharding import Mesh
from jax.sharding import PartitionSpec as P

FIRST = ("y", "x", "zh")
SECOND = ("zm", "zq", "c")
PLANE = ("y", "x")
f32, bf16 = jnp.float32, jnp.bfloat16
VMEM = pl.BlockSpec(memory_space=pltpu.VMEM)
SMEM = pl.BlockSpec(memory_space=pltpu.SMEM)
HBM = pl.BlockSpec(memory_space=pltpu.HBM)


def from_everyone(shard, axis):
    peers = lax.axis_size(axis)
    return lax.all_to_all(
        jnp.broadcast_to(shard[None], (peers, *shard.shape)), axis, 0, 0, tiled=True
    )


def swapped(shard, axis):
    return lax.ppermute(shard, axis, [(0, 1), (1, 0)])


def couplings(row, times):
    wide = jnp.broadcast_to(row, (32, 32))
    at_row = lax.broadcasted_iota(jnp.int32, (32, 32), 0)
    at_lane = lax.broadcasted_iota(jnp.int32, (32, 32), 1)
    column = jnp.sum(jnp.where(at_row == at_lane, wide, 0.0), axis=1, keepdims=True)
    tile = jnp.concatenate([column * wide] * 4, axis=1)
    return jnp.concatenate([tile] * times, axis=0)


def spectral(less_re, less_im, great_re, great_im, factor):
    lsquare_re = less_re * less_re - less_im * less_im
    lsquare_im = 2.0 * less_re * less_im
    gsquare_re = great_re * great_re - great_im * great_im
    gsquare_im = 2.0 * great_re * great_im
    real = (lsquare_re * great_re + lsquare_im * great_im) - (
        gsquare_re * less_re + gsquare_im * less_im
    )
    imag = (lsquare_im * great_re - lsquare_re * great_im) - (
        gsquare_im * less_re - gsquare_re * less_im
    )
    return factor * real, factor * imag


def dot(left, right):
    return jnp.dot(left, right, preferred_element_type=f32)


def compose(window_ref, damp_ref, coupling_ref, out_ref):
    fields = [[window_ref[which, part] for part in range(2)] for which in range(2)]
    for which in range(2):
        for part in range(2):
            start = 128 * which + 64 * part
            out_ref[start : start + 64] = fields[which][part].astype(bf16)
    damp = damp_ref[...]
    high = damp.astype(bf16).astype(f32)
    mid = (damp - high).astype(bf16).astype(f32)
    low = damp - high - mid
    rows = jnp.concatenate([high, mid, low, jnp.zeros_like(low)], axis=1)
    out_ref[256:264] = jnp.concatenate([rows, jnp.zeros((6, 128), f32)], axis=0).astype(bf16)
    real, imag = spectral(*fields[0], *fields[1], couplings(coupling_ref[...], 2))
    out_ref[264:328], out_ref[328:392] = real.astype(bf16), imag.astype(bf16)


def row_times_column(pieces, y_ref, acc_ref):
    for n, (left, blocks) in enumerate(pieces):
        right = [
            jnp.concatenate(
                [y_ref[j, :, 0:64].reshape(128, 128), y_ref[j, :, 64:128].reshape(128, 128)],
                axis=1,
            )
            for j in blocks
        ]
        part = dot(jnp.concatenate(left, axis=1), jnp.concatenate(right, axis=0))
        if n == 0:
            acc_ref[...] = part
        else:
            acc_ref[...] += part


def first_collision(scale, where_ref, own_ref, other_ref, y_ref, out_ref, acc_ref):
    core = where_ref[2]
    pieces = [
        (
            [s_ref[q, m].reshape(256, 128) for m in range(2)],
            [8 * m + 2 * q + side for m in range(2)],
        )
        for s_ref, side in ((own_ref, core), (other_ref, 1 - core))
        for q in range(4)
    ]
    row_times_column(pieces, y_ref, acc_ref)
    for h in range(2):
        top, low = acc_ref[h * 128 : h * 128 + 64], acc_ref[h * 128 + 64 : h * 128 + 128]
        real = (scale * (top[:, :128] - low[:, 128:])).astype(bf16)
        imag = (scale * (top[:, 128:] + low[:, :128])).astype(bf16)
        for peer in range(16):
            out_ref[peer, h, 0:64] = real
            out_ref[peer, h, 64:128] = imag


def last_collision(scale, s_ref, y_ref, base_ref, out_ref, acc_ref):
    pieces = [
        ([s_ref[side, q, m] for m in range(2)], [8 * m + 2 * q + side for m in range(2)])
        for side in range(2)
        for q in range(4)
    ]
    row_times_column(pieces, y_ref, acc_ref)
    top, low = acc_ref[0:64], acc_ref[64:128]
    out_ref[0] = base_ref[0:64] + (0.5 * scale) * (top[:, :128] - low[:, 128:])
    out_ref[1] = base_ref[64:128] + (0.5 * scale) * (top[:, 128:] + low[:, :128])


def halves(x):
    high = x.astype(bf16)
    return high, (x - high.astype(f32)).astype(bf16)


def long_product(left, right):
    lh, ll = left
    rh, rl = halves(right)
    return dot(
        jnp.concatenate([lh, lh, ll, ll], axis=1), jnp.concatenate([rh, rl, rh, rl], axis=0)
    )


def embedded(z):
    return jnp.concatenate([z, jnp.concatenate([-z[32:], z[:32]], axis=0)], axis=1)


def put_unit(z, at):
    row = lax.broadcasted_iota(jnp.int32, z.shape, 0)
    lane = lax.broadcasted_iota(jnp.int32, z.shape, 1)
    unit = jnp.where((row == lane - 32 * at) & (row < 32), 1.0, 0.0)
    return jnp.where(lane >= 32 * at, unit, z)


def lanes_from_zero(z, last):
    moved = jnp.concatenate([z[:, 32:], z[:, :32]], axis=1)
    row = lax.broadcasted_iota(jnp.int32, z.shape, 0)
    lane = lax.broadcasted_iota(jnp.int32, z.shape, 1)
    tail = jnp.where(row == lane - 224, 1.0, 0.0) if last else jnp.zeros_like(z)
    return jnp.where(lane >= 224, tail, moved)


def build_steps(damp_ref, u_ref, out_hbm, p_ref, last_ref, pc_ref, z_ref, sems):
    copies = [
        pltpu.make_async_copy(p_ref.at[k], out_hbm.at[k, 0:512, 0:640], sems.at[k])
        for k in range(8)
    ]
    copies.append(pltpu.make_async_copy(last_ref, out_hbm.at[:, 512:640, 0:256], sems.at[8]))
    copies.append(pltpu.make_async_copy(pc_ref, out_hbm.at[:, 640:704, 0:896], sems.at[9]))
    left = halves(embedded(u_ref[...]))

    def store(k, i, z):
        high, low = halves(lanes_from_zero(z, i == 7))
        first_high, first_low = halves(z[:, :32])
        first = jnp.concatenate([first_high, first_high, first_low], axis=1)
        for part in range(2):
            start = 256 * part + 32 * i
            rows, to = slice(32 * part, 32 * part + 32), slice(start, start + 32)
            p_ref[k, to, 0:256] = high[rows]
            p_ref[k, to, 256:512] = low[rows]
            p_ref[k, to, 512:608] = first[rows]
            if i == 7:
                last_ref[k, rows] = high[rows]
                last_ref[k, 64 + 32 * part : 96 + 32 * part] = low[rows]

    for k in range(8):
        start = jnp.concatenate([u_ref[...], jnp.zeros((64, 224), f32)], axis=1)
        z = put_unit(damp_ref[:, 8 * k : 8 * k + 1] * start, 1)
        z_ref[k] = z
        store(k, 0, z)
    for i in range(1, 8):
        for k in range(8):
            t = 8 * k + i
            z = damp_ref[:, t : t + 1] * long_product(left, z_ref[k])
            if i < 7:
                z = put_unit(z, i + 1)
            z_ref[k] = z
            store(k, i, z)
            if i == 7:
                copies[k].start()
    copies[8].start()

    w = None
    for k in range(8):
        whole = z_ref[k][:, :32]
        if k == 0:
            w = put_unit(jnp.concatenate([whole, jnp.zeros((64, 224), f32)], axis=1), 1)
        else:
            w = long_product(halves(embedded(whole)), w)
            if k < 7:
                w = put_unit(w, k + 1)
        high, low = halves(lanes_from_zero(w, k == 7))
        pc_ref[k, :, 0:256] = high
        pc_ref[k, :, 256:512] = high
        pc_ref[k, :, 512:768] = low
        pc_ref[k, :, 768:832] = jnp.concatenate(halves(w[:, :32]), axis=1)
    copies[9].start()
    for copy in copies:
        copy.wait()


def predict(
    where_ref, force_ref, lg_ref, coupling_ref, plan_hbm,
    y_ref, t_ref, base_ref,
    p_ref, last_ref, pc_ref, f_ref, s_ref, ends_ref, carry_ref, hom_ref, x_ref, sems,
):
    copies = [
        pltpu.make_async_copy(plan_hbm.at[:, 512:640, 0:256], last_ref, sems.at[8]),
        pltpu.make_async_copy(plan_hbm.at[:, 640:704, 0:896], pc_ref, sems.at[9]),
    ]

    def fetch(k):
        return pltpu.make_async_copy(
            plan_hbm.at[k, 0:512, 0:640], p_ref.at[k], sems.at[k]
        )

    for copy in copies + [fetch(k) for k in range(8)]:
        copy.start()

    j, h = where_ref[0], where_ref[1]
    own_block, own_start = j // 2, pl.multiple_of((j % 2) * 128 + h * 64, 64)
    own_low = pl.multiple_of(own_start + 256, 64)

    def block_of(ref, k, start):
        return jnp.concatenate(
            [
                jnp.concatenate(
                    [
                        ref[2 * k + u // 2, u % 2, start + 64 * part : start + 64 * part + 64]
                        for u in range(4)
                    ],
                    axis=0,
                )
                for part in range(2)
            ],
            axis=1,
        )

    def parts(product):
        rows = product.shape[0] // 2
        top, low = product[:rows], product[rows:]
        return top[:, :128] - low[:, 128:], top[:, 128:] + low[:, :128]

    def twice(x):
        return jnp.concatenate([x, x], axis=0)

    def put_end(k, source):
        product = dot(last_ref[k], source)
        real, imag = parts(product[:64] + product[64:])
        high, low = halves(jnp.concatenate([real, imag], axis=1))
        ends_ref[0, k], ends_ref[1, k], ends_ref[2, k] = high, low, high

    def coarse():
        return dot(pc_ref[:, :, 0:768].reshape(512, 768), ends_ref[...].reshape(768, 256))

    def rows_of(product, k):
        part = product[k * 64 : k * 64 + 64]
        return jnp.concatenate(parts(part), axis=1)

    def triple(x):
        high, low = halves(x)
        return jnp.concatenate([high, low, high], axis=0)

    for k in range(8):
        f_ref[k] = block_of(force_ref, k, 0)
    copies[0].wait()
    for k in range(8):
        put_end(k, f_ref[k])
    copies[1].wait()
    initial = jnp.concatenate([lg_ref[0, 0, 0:32], lg_ref[0, 0, 64:96]], axis=1)
    hom = dot(pc_ref[:, :, 768:832].reshape(512, 64), twice(initial))
    carry = coarse() + hom
    hom_ref[0] = carry_ref[0] = triple(initial.astype(f32))
    for k in range(7):
        hom_ref[k + 1] = triple(rows_of(hom, k))
        carry_ref[k + 1] = triple(rows_of(carry, k))
    factor = couplings(coupling_ref[...], 2)

    def piece(k, u):
        n, row = 4 * k + u, u * 64

        width = 128 if u < 2 else 256
        rows = jnp.concatenate(
            [
                jnp.concatenate(
                    [p_ref[k, at : at + 64, lane : lane + width] for lane in (0, 256)]
                    + [p_ref[k, at : at + 64, 512:608]],
                    axis=1,
                )
                for at in (row, row + 256)
            ],
            axis=0,
        )
        force = f_ref[k, 0:width]
        source = jnp.concatenate([force, force, carry_ref[k]], axis=0)
        real, imag = parts(dot(rows, source))
        j_at, h_at = 2 * k + u // 2, u % 2
        g = lg_ref[j_at, h_at, 128:256].astype(f32)
        spectral_re, spectral_im = spectral(real, imag, g[:64], g[64:], factor)
        s = jnp.concatenate([spectral_re, spectral_im], axis=1).astype(bf16)
        s_ref[k, pl.ds(row, 64)] = s
        y_ref[j_at, h_at, 0:64] = real.astype(bf16)
        y_ref[j_at, h_at, 64:128] = imag.astype(bf16)
        x_ref[n, 0:64], x_ref[n, 64:128] = real, imag

    def block(k, _):
        fetch(k).wait()
        for u in range(4):
            piece(k, u)
        return 0

    lax.fori_loop(0, 8, block, 0)
    for k in range(8):
        put_end(k, s_ref[k])
    carry = coarse()
    carry_ref[0] = jnp.zeros((96, 256), bf16)
    for k in range(7):
        carry_ref[k + 1] = triple(rows_of(carry, k))

    def own(ref):
        return jnp.concatenate(
            [ref[own_block, pl.ds(own_start, 64)], ref[own_block, pl.ds(own_low, 64)]], axis=0
        )

    p_own, s_own = own(p_ref), s_ref[own_block]
    source = jnp.concatenate([s_own, s_own, carry_ref[own_block]], axis=0)
    real, imag = parts(dot(p_own[:, 0:608], source))
    t_ref[0:64], t_ref[64:128] = real.astype(bf16), imag.astype(bf16)
    real, imag = parts(dot(p_own[:, 512:608], hom_ref[own_block]))
    base = x_ref[2 * j + h]
    base_ref[0:64] = 0.5 * (base[0:64] + real)
    base_ref[64:128] = 0.5 * (base[64:128] + imag)


PRED_SCRATCH = [
    pltpu.VMEM((8, 512, 640), bf16),
    pltpu.VMEM((8, 128, 256), bf16),
    pltpu.VMEM((8, 64, 896), bf16),
    pltpu.VMEM((8, 256, 256), bf16),
    pltpu.VMEM((8, 256, 256), bf16),
    pltpu.VMEM((3, 8, 32, 256), bf16),
    pltpu.VMEM((8, 96, 256), bf16),
    pltpu.VMEM((8, 96, 256), bf16),
    pltpu.VMEM((32, 128, 128), f32),
    pltpu.SemaphoreType.DMA((10,)),
]


def call(kernel, outs, scratch, ins, flops, moved, grant=24, place=VMEM):
    return pl.pallas_call(
        kernel,
        out_shape=outs,
        in_specs=ins,
        out_specs=jax.tree.map(lambda _: place, outs),
        scratch_shapes=scratch,
        compiler_params=pltpu.CompilerParams(vmem_limit_bytes=int(grant * (1 << 20))),
        cost_estimate=pl.CostEstimate(flops=flops, bytes_accessed=moved, transcendentals=0),
    )


def shape(*dims, kind=bf16):
    return jax.ShapeDtypeStruct(dims, kind)


def shards(window, damping, propagator, coupling):
    orbitals = coupling.shape[0]
    horizon = damping.shape[0] * lax.axis_size(FIRST)
    scale = 1.0 / (horizon * math.sqrt(orbitals))
    where = jnp.stack([lax.axis_index(axis) for axis in (PLANE, "zh", "c")]).astype(jnp.int32)

    strength = coupling.reshape(1, 32)
    message = call(
        compose,
        shape(392, 128),
        [],
        [VMEM, VMEM, VMEM],
        40 * 64 * 128,
        400 << 10,
        63.9,
    )(window.reshape(2, 2, 64, 128), damping, strength)
    pair = lax.all_gather(message, "zh")
    lg = from_everyone(pair[:, :264], PLANE)

    s_rows = lax.all_gather(pair[:, 264:], "zm")
    s_rows = lax.all_gather(s_rows, "zq")
    s_other = swapped(s_rows, "c")

    c1 = call(
        functools.partial(first_collision, scale),
        shape(16, 2, 128, 128),
        [pltpu.VMEM((256, 256), f32)],
        [SMEM, VMEM, VMEM, VMEM],
        2 * 256 * 256 * 2048,
        4 << 20,
    )(where, s_rows, s_other, lg)
    force = lax.all_to_all(c1, PLANE, 0, 0, tiled=True)

    parts = lg[:, :, 256:258].reshape(64, 128).astype(f32)
    damp = parts[:, 0:32] + (parts[:, 32:64] + parts[:, 64:96])
    damp = jnp.tile(damp.T, (2, 1))
    plan = call(
        build_steps,
        shape(8, 704, 1024),
        [
            pltpu.VMEM((8, 512, 640), bf16),
            pltpu.VMEM((8, 128, 256), bf16),
            pltpu.VMEM((8, 64, 896), bf16),
            pltpu.VMEM((8, 64, 256), f32),
            pltpu.SemaphoreType.DMA((10,)),
        ],
        [VMEM, VMEM],
        64 * 2 * 64 * 256 * 256,
        6 << 20,
        54,
        HBM,
    )(damp, propagator.reshape(64, 32))

    y2, t2, base = call(
        predict,
        (shape(16, 2, 128, 128), shape(128, 128), shape(128, 128, kind=f32)),
        PRED_SCRATCH,
        [SMEM] + [VMEM] * 3 + [HBM],
        2 * 8 * 512 * 512 * 128 * 2,
        10 << 20,
        44,
    )(where, force, lg, strength, plan)

    t_rows = from_everyone(lax.all_gather(t2, "zm"), "zq")
    t_rows = lax.all_gather(t_rows, "c")
    out = call(
        functools.partial(last_collision, scale),
        shape(2, 64, 128, kind=f32),
        [pltpu.VMEM((128, 256), f32)],
        [VMEM, VMEM, VMEM],
        2 * 128 * 256 * 2048,
        2 << 20,
    )(t_rows, y2, base)
    return out.reshape(2, 2, orbitals, 128)


def solution(mesh):
    finer = Mesh(mesh.devices.reshape(4, 4, 2, 2, 4, 2), (*FIRST, *SECOND))
    placed = (P(None, None, FIRST, None, SECOND), P(FIRST, None), P(), P())
    return jax.shard_map(
        shards, mesh=finer, in_specs=placed, out_specs=P(None, FIRST, None, SECOND), check_vma=False
    )
```

```python
import functools
import math

import jax
import jax.numpy as jnp
from jax import lax
from jax.experimental import pallas as pl
from jax.experimental.pallas import tpu as pltpu
from jax.sharding import Mesh
from jax.sharding import PartitionSpec as P

FIRST = ("y", "x", "zh")
SECOND = ("zm", "zq", "c")
PLANE = ("y", "x")
f32, bf16 = jnp.float32, jnp.bfloat16
VMEM = pl.BlockSpec(memory_space=pltpu.VMEM)
HBM = pl.BlockSpec(memory_space=pltpu.HBM)


def from_everyone(shard, axis):
    peers = lax.axis_size(axis)
    return lax.all_to_all(
        jnp.broadcast_to(shard[None], (peers, *shard.shape)), axis, 0, 0, tiled=True
    )


def swapped(shard, axis):
    return lax.ppermute(shard, axis, [(0, 1), (1, 0)])


def couplings(row, times):
    wide = jnp.broadcast_to(row, (32, 32))
    at_row = lax.broadcasted_iota(jnp.int32, (32, 32), 0)
    at_lane = lax.broadcasted_iota(jnp.int32, (32, 32), 1)
    column = jnp.sum(jnp.where(at_row == at_lane, wide, 0.0), axis=1, keepdims=True)
    tile = jnp.concatenate([column * wide] * 4, axis=1)
    return jnp.concatenate([tile] * times, axis=0)


def spectral(less_re, less_im, great_re, great_im, factor):
    lsquare_re = less_re * less_re - less_im * less_im
    lsquare_im = 2.0 * less_re * less_im
    gsquare_re = great_re * great_re - great_im * great_im
    gsquare_im = 2.0 * great_re * great_im
    real = (lsquare_re * great_re + lsquare_im * great_im) - (
        gsquare_re * less_re + gsquare_im * less_im
    )
    imag = (lsquare_im * great_re - lsquare_re * great_im) - (
        gsquare_im * less_re - gsquare_re * less_im
    )
    return factor * real, factor * imag


def dot(left, right):
    return jnp.dot(left, right, preferred_element_type=f32)


def compose(window_ref, damp_ref, coupling_ref, out_ref):
    fields = [[window_ref[which, part] for part in range(2)] for which in range(2)]
    for which in range(2):
        for part in range(2):
            start = 128 * which + 64 * part
            out_ref[start : start + 64] = fields[which][part].astype(bf16)
    damp = damp_ref[...]
    high = damp.astype(bf16).astype(f32)
    mid = (damp - high).astype(bf16).astype(f32)
    low = damp - high - mid
    rows = jnp.concatenate([high, mid, low, jnp.zeros_like(low)], axis=1)
    out_ref[256:264] = jnp.concatenate([rows, jnp.zeros((6, 128), f32)], axis=0).astype(bf16)
    real, imag = spectral(*fields[0], *fields[1], couplings(coupling_ref[...], 2))
    out_ref[264:328], out_ref[328:392] = real.astype(bf16), imag.astype(bf16)


def row_times_column(pieces, y_ref, acc_ref):
    for n, (left, blocks) in enumerate(pieces):
        right = [
            jnp.concatenate(
                [y_ref[j, :, 0:64].reshape(128, 128), y_ref[j, :, 64:128].reshape(128, 128)],
                axis=1,
            )
            for j in blocks
        ]
        part = dot(jnp.concatenate(left, axis=1), jnp.concatenate(right, axis=0))
        if n == 0:
            acc_ref[...] = part
        else:
            acc_ref[...] += part


def first_collision(scale, own_ref, other_ref, y_ref, out_ref, acc_ref):
    core = lax.axis_index("c")
    pieces = [
        (
            [s_ref[q, m].reshape(256, 128) for m in range(2)],
            [8 * m + 2 * q + side for m in range(2)],
        )
        for s_ref, side in ((own_ref, core), (other_ref, 1 - core))
        for q in range(4)
    ]
    row_times_column(pieces, y_ref, acc_ref)
    for h in range(2):
        top, low = acc_ref[h * 128 : h * 128 + 64], acc_ref[h * 128 + 64 : h * 128 + 128]
        real = (scale * (top[:, :128] - low[:, 128:])).astype(bf16)
        imag = (scale * (top[:, 128:] + low[:, :128])).astype(bf16)
        for peer in range(16):
            out_ref[peer, h, 0:64] = real
            out_ref[peer, h, 64:128] = imag


def last_collision(scale, s_ref, y_ref, base_ref, out_ref, acc_ref):
    pieces = [
        ([s_ref[side, q, m] for m in range(2)], [8 * m + 2 * q + side for m in range(2)])
        for side in range(2)
        for q in range(4)
    ]
    row_times_column(pieces, y_ref, acc_ref)
    top, low = acc_ref[0:64], acc_ref[64:128]
    out_ref[0] = base_ref[0:64] + (0.5 * scale) * (top[:, :128] - low[:, 128:])
    out_ref[1] = base_ref[64:128] + (0.5 * scale) * (top[:, 128:] + low[:, :128])


def halves(x):
    high = x.astype(bf16)
    return high, (x - high.astype(f32)).astype(bf16)


def long_product(left, right):
    lh, ll = left
    rh, rl = halves(right)
    return dot(
        jnp.concatenate([lh, lh, ll, ll], axis=1), jnp.concatenate([rh, rl, rh, rl], axis=0)
    )


def embedded(z):
    return jnp.concatenate([z, jnp.concatenate([-z[32:], z[:32]], axis=0)], axis=1)


def put_unit(z, at):
    row = lax.broadcasted_iota(jnp.int32, z.shape, 0)
    lane = lax.broadcasted_iota(jnp.int32, z.shape, 1)
    unit = jnp.where((row == lane - 32 * at) & (row < 32), 1.0, 0.0)
    return jnp.where(lane >= 32 * at, unit, z)


def lanes_from_zero(z, last):
    moved = jnp.concatenate([z[:, 32:], z[:, :32]], axis=1)
    row = lax.broadcasted_iota(jnp.int32, z.shape, 0)
    lane = lax.broadcasted_iota(jnp.int32, z.shape, 1)
    tail = jnp.where(row == lane - 224, 1.0, 0.0) if last else jnp.zeros_like(z)
    return jnp.where(lane >= 224, tail, moved)


def build_steps(damp_ref, u_ref, out_hbm, p_ref, last_ref, pc_ref, z_ref, sems):
    copies = [
        pltpu.make_async_copy(p_ref.at[k], out_hbm.at[k, 0:512, 0:640], sems.at[k])
        for k in range(8)
    ]
    copies.append(pltpu.make_async_copy(last_ref, out_hbm.at[:, 512:640, 0:256], sems.at[8]))
    copies.append(pltpu.make_async_copy(pc_ref, out_hbm.at[:, 640:704, 0:896], sems.at[9]))
    left = halves(embedded(u_ref[...]))

    def store(k, i, z):
        high, low = halves(lanes_from_zero(z, i == 7))
        first_high, first_low = halves(z[:, :32])
        first = jnp.concatenate([first_high, first_high, first_low], axis=1)
        for part in range(2):
            start = 256 * part + 32 * i
            rows, to = slice(32 * part, 32 * part + 32), slice(start, start + 32)
            p_ref[k, to, 0:256] = high[rows]
            p_ref[k, to, 256:512] = low[rows]
            p_ref[k, to, 512:608] = first[rows]
            if i == 7:
                last_ref[k, rows] = high[rows]
                last_ref[k, 64 + 32 * part : 96 + 32 * part] = low[rows]

    for k in range(8):
        start = jnp.concatenate([u_ref[...], jnp.zeros((64, 224), f32)], axis=1)
        z = put_unit(damp_ref[:, 8 * k : 8 * k + 1] * start, 1)
        z_ref[k] = z
        store(k, 0, z)
    for i in range(1, 8):
        for k in range(8):
            t = 8 * k + i
            z = damp_ref[:, t : t + 1] * long_product(left, z_ref[k])
            if i < 7:
                z = put_unit(z, i + 1)
            z_ref[k] = z
            store(k, i, z)
            if i == 7:
                copies[k].start()
    copies[8].start()

    w = None
    for k in range(8):
        whole = z_ref[k][:, :32]
        if k == 0:
            w = put_unit(jnp.concatenate([whole, jnp.zeros((64, 224), f32)], axis=1), 1)
        else:
            w = long_product(halves(embedded(whole)), w)
            if k < 7:
                w = put_unit(w, k + 1)
        high, low = halves(lanes_from_zero(w, k == 7))
        pc_ref[k, :, 0:256] = high
        pc_ref[k, :, 256:512] = high
        pc_ref[k, :, 512:768] = low
        pc_ref[k, :, 768:832] = jnp.concatenate(halves(w[:, :32]), axis=1)
    copies[9].start()
    for copy in copies:
        copy.wait()


def predict(
    force_ref, lg_ref, coupling_ref, plan_hbm,
    y_ref, t_ref, base_ref,
    p_ref, last_ref, pc_ref, f_ref, s_ref, ends_ref, carry_ref, hom_ref, x_ref, sems,
):
    copies = [
        pltpu.make_async_copy(plan_hbm.at[:, 512:640, 0:256], last_ref, sems.at[8]),
        pltpu.make_async_copy(plan_hbm.at[:, 640:704, 0:896], pc_ref, sems.at[9]),
    ]

    def fetch(k):
        return pltpu.make_async_copy(
            plan_hbm.at[k, 0:512, 0:640], p_ref.at[k], sems.at[k]
        )

    for copy in copies + [fetch(k) for k in range(8)]:
        copy.start()

    j = lax.axis_index("y") * lax.axis_size("x") + lax.axis_index("x")
    h = lax.axis_index("zh")
    own_block, own_start = j // 2, pl.multiple_of((j % 2) * 128 + h * 64, 64)
    own_low = pl.multiple_of(own_start + 256, 64)

    def block_of(ref, k, start):
        return jnp.concatenate(
            [
                jnp.concatenate(
                    [
                        ref[2 * k + u // 2, u % 2, start + 64 * part : start + 64 * part + 64]
                        for u in range(4)
                    ],
                    axis=0,
                )
                for part in range(2)
            ],
            axis=1,
        )

    def parts(product):
        rows = product.shape[0] // 2
        top, low = product[:rows], product[rows:]
        return top[:, :128] - low[:, 128:], top[:, 128:] + low[:, :128]

    def twice(x):
        return jnp.concatenate([x, x], axis=0)

    def put_end(k, source):
        product = dot(last_ref[k], source)
        real, imag = parts(product[:64] + product[64:])
        high, low = halves(jnp.concatenate([real, imag], axis=1))
        ends_ref[0, k], ends_ref[1, k], ends_ref[2, k] = high, low, high

    def coarse():
        return dot(pc_ref[:, :, 0:768].reshape(512, 768), ends_ref[...].reshape(768, 256))

    def rows_of(product, k):
        part = product[k * 64 : k * 64 + 64]
        return jnp.concatenate(parts(part), axis=1)

    def triple(x):
        high, low = halves(x)
        return jnp.concatenate([high, low, high], axis=0)

    for k in range(8):
        f_ref[k] = block_of(force_ref, k, 0)
    copies[0].wait()
    for k in range(8):
        put_end(k, f_ref[k])
    copies[1].wait()
    initial = jnp.concatenate([lg_ref[0, 0, 0:32], lg_ref[0, 0, 64:96]], axis=1)
    hom = dot(pc_ref[:, :, 768:832].reshape(512, 64), twice(initial))
    carry = coarse() + hom
    hom_ref[0] = carry_ref[0] = triple(initial.astype(f32))
    for k in range(7):
        hom_ref[k + 1] = triple(rows_of(hom, k))
        carry_ref[k + 1] = triple(rows_of(carry, k))
    factor = couplings(coupling_ref[...], 2)

    def piece(k, u):
        n, row = 4 * k + u, u * 64

        width = 128 if u < 2 else 256
        rows = jnp.concatenate(
            [
                jnp.concatenate(
                    [p_ref[k, at : at + 64, lane : lane + width] for lane in (0, 256)]
                    + [p_ref[k, at : at + 64, 512:608]],
                    axis=1,
                )
                for at in (row, row + 256)
            ],
            axis=0,
        )
        force = f_ref[k, 0:width]
        source = jnp.concatenate([force, force, carry_ref[k]], axis=0)
        real, imag = parts(dot(rows, source))
        j_at, h_at = 2 * k + u // 2, u % 2
        g = lg_ref[j_at, h_at, 128:256].astype(f32)
        spectral_re, spectral_im = spectral(real, imag, g[:64], g[64:], factor)
        s = jnp.concatenate([spectral_re, spectral_im], axis=1).astype(bf16)
        s_ref[k, pl.ds(row, 64)] = s
        y_ref[j_at, h_at, 0:64] = real.astype(bf16)
        y_ref[j_at, h_at, 64:128] = imag.astype(bf16)
        x_ref[n, 0:64], x_ref[n, 64:128] = real, imag

    def block(k, _):
        fetch(k).wait()
        for u in range(4):
            piece(k, u)
        return 0

    lax.fori_loop(0, 8, block, 0)
    for k in range(8):
        put_end(k, s_ref[k])
    carry = coarse()
    carry_ref[0] = jnp.zeros((96, 256), bf16)
    for k in range(7):
        carry_ref[k + 1] = triple(rows_of(carry, k))

    def own(ref):
        return jnp.concatenate(
            [ref[own_block, pl.ds(own_start, 64)], ref[own_block, pl.ds(own_low, 64)]], axis=0
        )

    p_own, s_own = own(p_ref), s_ref[own_block]
    source = jnp.concatenate([s_own, s_own, carry_ref[own_block]], axis=0)
    real, imag = parts(dot(p_own[:, 0:608], source))
    t_ref[0:64], t_ref[64:128] = real.astype(bf16), imag.astype(bf16)
    real, imag = parts(dot(p_own[:, 512:608], hom_ref[own_block]))
    base = x_ref[2 * j + h]
    base_ref[0:64] = 0.5 * (base[0:64] + real)
    base_ref[64:128] = 0.5 * (base[64:128] + imag)


PRED_SCRATCH = [
    pltpu.VMEM((8, 512, 640), bf16),
    pltpu.VMEM((8, 128, 256), bf16),
    pltpu.VMEM((8, 64, 896), bf16),
    pltpu.VMEM((8, 256, 256), bf16),
    pltpu.VMEM((8, 256, 256), bf16),
    pltpu.VMEM((3, 8, 32, 256), bf16),
    pltpu.VMEM((8, 96, 256), bf16),
    pltpu.VMEM((8, 96, 256), bf16),
    pltpu.VMEM((32, 128, 128), f32),
    pltpu.SemaphoreType.DMA((10,)),
]


def call(kernel, outs, scratch, ins, flops, moved, grant=24, place=VMEM):
    return pl.pallas_call(
        kernel,
        out_shape=outs,
        in_specs=ins,
        out_specs=jax.tree.map(lambda _: place, outs),
        scratch_shapes=scratch,
        compiler_params=pltpu.CompilerParams(vmem_limit_bytes=int(grant * (1 << 20))),
        cost_estimate=pl.CostEstimate(flops=flops, bytes_accessed=moved, transcendentals=0),
    )


def shape(*dims, kind=bf16):
    return jax.ShapeDtypeStruct(dims, kind)


def shards(window, damping, propagator, coupling):
    orbitals = coupling.shape[0]
    horizon = damping.shape[0] * lax.axis_size(FIRST)
    scale = 1.0 / (horizon * math.sqrt(orbitals))
    strength = coupling.reshape(1, 32)
    message = call(
        compose,
        shape(392, 128),
        [],
        [VMEM, VMEM, VMEM],
        40 * 64 * 128,
        400 << 10,
        63.9,
    )(window.reshape(2, 2, 64, 128), damping, strength)
    pair = lax.all_gather(message, "zh")
    lg = from_everyone(pair[:, :264], PLANE)

    s_rows = lax.all_gather(pair[:, 264:], "zm")
    s_rows = lax.all_gather(s_rows, "zq")
    s_other = swapped(s_rows, "c")

    c1 = call(
        functools.partial(first_collision, scale),
        shape(16, 2, 128, 128),
        [pltpu.VMEM((256, 256), f32)],
        [VMEM, VMEM, VMEM],
        2 * 256 * 256 * 2048,
        4 << 20,
    )(s_rows, s_other, lg)
    force = lax.all_to_all(c1, PLANE, 0, 0, tiled=True)

    parts = lg[:, :, 256:258].reshape(64, 128).astype(f32)
    damp = parts[:, 0:32] + (parts[:, 32:64] + parts[:, 64:96])
    damp = jnp.tile(damp.T, (2, 1))
    plan = call(
        build_steps,
        shape(8, 704, 1024),
        [
            pltpu.VMEM((8, 512, 640), bf16),
            pltpu.VMEM((8, 128, 256), bf16),
            pltpu.VMEM((8, 64, 896), bf16),
            pltpu.VMEM((8, 64, 256), f32),
            pltpu.SemaphoreType.DMA((10,)),
        ],
        [VMEM, VMEM],
        64 * 2 * 64 * 256 * 256,
        6 << 20,
        54,
        HBM,
    )(damp, propagator.reshape(64, 32))

    y2, t2, base = call(
        predict,
        (shape(16, 2, 128, 128), shape(128, 128), shape(128, 128, kind=f32)),
        PRED_SCRATCH,
        [VMEM] * 3 + [HBM],
        2 * 8 * 512 * 512 * 128 * 2,
        10 << 20,
        44,
    )(force, lg, strength, plan)

    t_rows = from_everyone(lax.all_gather(t2, "zm"), "zq")
    t_rows = lax.all_gather(t_rows, "c")
    out = call(
        functools.partial(last_collision, scale),
        shape(2, 64, 128, kind=f32),
        [pltpu.VMEM((128, 256), f32)],
        [VMEM, VMEM, VMEM],
        2 * 128 * 256 * 2048,
        2 << 20,
    )(t_rows, y2, base)
    return out.reshape(2, 2, orbitals, 128)


def solution(mesh):
    finer = Mesh(mesh.devices.reshape(4, 4, 2, 2, 4, 2), (*FIRST, *SECOND))
    placed = (P(None, None, FIRST, None, SECOND), P(FIRST, None), P(), P())
    return jax.shard_map(
        shards, mesh=finer, in_specs=placed, out_specs=P(None, FIRST, None, SECOND), check_vma=False
    )
```

```python
import functools
import math

import jax
import jax.numpy as jnp
from jax import lax
from jax.experimental import pallas as pl
from jax.experimental.pallas import tpu as pltpu
from jax.sharding import Mesh
from jax.sharding import PartitionSpec as P

FIRST = ("y", "x", "zh")
SECOND = ("zm", "zq", "c")
PLANE = ("y", "x")
f32, bf16 = jnp.float32, jnp.bfloat16
VMEM = pl.BlockSpec(memory_space=pltpu.VMEM)
HBM = pl.BlockSpec(memory_space=pltpu.HBM)


def from_everyone(shard, axis):
    peers = lax.axis_size(axis)
    return lax.all_to_all(
        jnp.broadcast_to(shard[None], (peers, *shard.shape)), axis, 0, 0, tiled=True
    )


def swapped(shard, axis):
    return lax.ppermute(shard, axis, [(0, 1), (1, 0)])


def couplings(row, times):
    wide = jnp.broadcast_to(row, (32, 32))
    at_row = lax.broadcasted_iota(jnp.int32, (32, 32), 0)
    at_lane = lax.broadcasted_iota(jnp.int32, (32, 32), 1)
    column = jnp.sum(jnp.where(at_row == at_lane, wide, 0.0), axis=1, keepdims=True)
    tile = jnp.concatenate([column * wide] * 4, axis=1)
    return jnp.concatenate([tile] * times, axis=0)


def spectral(less_re, less_im, great_re, great_im, factor):
    lsquare_re = less_re * less_re - less_im * less_im
    lsquare_im = 2.0 * less_re * less_im
    gsquare_re = great_re * great_re - great_im * great_im
    gsquare_im = 2.0 * great_re * great_im
    real = (lsquare_re * great_re + lsquare_im * great_im) - (
        gsquare_re * less_re + gsquare_im * less_im
    )
    imag = (lsquare_im * great_re - lsquare_re * great_im) - (
        gsquare_im * less_re - gsquare_re * less_im
    )
    return factor * real, factor * imag


def dot(left, right):
    return jnp.dot(left, right, preferred_element_type=f32)


def compose(window_ref, damp_ref, coupling_ref, out_ref):
    fields = [[window_ref[which, part] for part in range(2)] for which in range(2)]
    for which in range(2):
        for part in range(2):
            start = 128 * which + 64 * part
            out_ref[start : start + 64] = fields[which][part].astype(bf16)
    damp = damp_ref[...]
    high = damp.astype(bf16).astype(f32)
    mid = (damp - high).astype(bf16).astype(f32)
    low = damp - high - mid
    rows = jnp.concatenate([high, mid, low, jnp.zeros_like(low)], axis=1)
    out_ref[256:264] = jnp.concatenate([rows, jnp.zeros((6, 128), f32)], axis=0).astype(bf16)
    real, imag = spectral(*fields[0], *fields[1], couplings(coupling_ref[...], 2))
    out_ref[264:328], out_ref[328:392] = real.astype(bf16), imag.astype(bf16)


def row_times_column(pieces, y_ref, acc_ref):
    for n, (left, blocks) in enumerate(pieces):
        right = [
            jnp.concatenate(
                [y_ref[j, :, 0:64].reshape(128, 128), y_ref[j, :, 64:128].reshape(128, 128)],
                axis=1,
            )
            for j in blocks
        ]
        part = dot(jnp.concatenate(left, axis=1), jnp.concatenate(right, axis=0))
        if n == 0:
            acc_ref[...] = part
        else:
            acc_ref[...] += part


def first_collision(scale, own_ref, other_ref, y_ref, out_ref, acc_ref):
    core = lax.axis_index("c")
    pieces = [
        (
            [s_ref[q, m].reshape(256, 128) for m in range(2)],
            [8 * m + 2 * q + side for m in range(2)],
        )
        for s_ref, side in ((own_ref, core), (other_ref, 1 - core))
        for q in range(4)
    ]
    row_times_column(pieces, y_ref, acc_ref)
    for h in range(2):
        top, low = acc_ref[h * 128 : h * 128 + 64], acc_ref[h * 128 + 64 : h * 128 + 128]
        real = (scale * (top[:, :128] - low[:, 128:])).astype(bf16)
        imag = (scale * (top[:, 128:] + low[:, :128])).astype(bf16)
        for peer in range(16):
            out_ref[peer, h, 0:64] = real
            out_ref[peer, h, 64:128] = imag


def last_collision(scale, s_ref, y_ref, base_ref, out_ref, acc_ref):
    pieces = [
        ([s_ref[side, q, m] for m in range(2)], [8 * m + 2 * q + side for m in range(2)])
        for side in range(2)
        for q in range(4)
    ]
    row_times_column(pieces, y_ref, acc_ref)
    top, low = acc_ref[0:64], acc_ref[64:128]
    out_ref[0] = base_ref[0:64] + (0.5 * scale) * (top[:, :128] - low[:, 128:])
    out_ref[1] = base_ref[64:128] + (0.5 * scale) * (top[:, 128:] + low[:, :128])


def halves(x):
    high = x.astype(bf16)
    return high, (x - high.astype(f32)).astype(bf16)


def long_product(left, right):
    lh, ll = left
    rh, rl = halves(right)
    return dot(
        jnp.concatenate([lh, lh, ll, ll], axis=1), jnp.concatenate([rh, rl, rh, rl], axis=0)
    )


def embedded(z):
    return jnp.concatenate([z, jnp.concatenate([-z[32:], z[:32]], axis=0)], axis=1)


def put_unit(z, at):
    row = lax.broadcasted_iota(jnp.int32, z.shape, 0)
    lane = lax.broadcasted_iota(jnp.int32, z.shape, 1)
    unit = jnp.where((row == lane - 32 * at) & (row < 32), 1.0, 0.0)
    return jnp.where(lane >= 32 * at, unit, z)


def lanes_from_zero(z, last):
    moved = jnp.concatenate([z[:, 32:], z[:, :32]], axis=1)
    row = lax.broadcasted_iota(jnp.int32, z.shape, 0)
    lane = lax.broadcasted_iota(jnp.int32, z.shape, 1)
    tail = jnp.where(row == lane - 224, 1.0, 0.0) if last else jnp.zeros_like(z)
    return jnp.where(lane >= 224, tail, moved)


def build_steps(damp_ref, u_ref, out_hbm, p_ref, last_ref, pc_ref, z_ref, sems):
    copies = [
        pltpu.make_async_copy(p_ref.at[k], out_hbm.at[k, 0:512, 0:640], sems.at[k])
        for k in range(8)
    ]
    copies.append(pltpu.make_async_copy(last_ref, out_hbm.at[:, 512:640, 0:256], sems.at[8]))
    copies.append(pltpu.make_async_copy(pc_ref, out_hbm.at[:, 640:704, 0:896], sems.at[9]))
    left = halves(embedded(u_ref[...]))

    def store(k, i, z):
        high, low = halves(lanes_from_zero(z, i == 7))
        first_high, first_low = halves(z[:, :32])
        first = jnp.concatenate([first_high, first_high, first_low], axis=1)
        for part in range(2):
            start = 256 * part + 32 * i
            rows, to = slice(32 * part, 32 * part + 32), slice(start, start + 32)
            p_ref[k, to, 0:256] = high[rows]
            p_ref[k, to, 256:512] = low[rows]
            p_ref[k, to, 512:608] = first[rows]
            if i == 7:
                last_ref[k, rows] = high[rows]
                last_ref[k, 64 + 32 * part : 96 + 32 * part] = low[rows]

    for k in range(8):
        start = jnp.concatenate([u_ref[...], jnp.zeros((64, 224), f32)], axis=1)
        z = put_unit(damp_ref[:, 8 * k : 8 * k + 1] * start, 1)
        z_ref[k] = z
        store(k, 0, z)
    for i in range(1, 8):
        for k in range(8):
            t = 8 * k + i
            z = damp_ref[:, t : t + 1] * long_product(left, z_ref[k])
            if i < 7:
                z = put_unit(z, i + 1)
            z_ref[k] = z
            store(k, i, z)
            if i == 7:
                copies[k].start()
    copies[8].start()

    w = None
    for k in range(8):
        whole = z_ref[k][:, :32]
        if k == 0:
            w = put_unit(jnp.concatenate([whole, jnp.zeros((64, 224), f32)], axis=1), 1)
        else:
            w = long_product(halves(embedded(whole)), w)
            if k < 7:
                w = put_unit(w, k + 1)
        high, low = halves(lanes_from_zero(w, k == 7))
        pc_ref[k, :, 0:256] = high
        pc_ref[k, :, 256:512] = high
        pc_ref[k, :, 512:768] = low
        pc_ref[k, :, 768:832] = jnp.concatenate(halves(w[:, :32]), axis=1)
    copies[9].start()
    for copy in copies:
        copy.wait()


def predict(
    force_ref, lg_ref, coupling_ref, plan_hbm,
    y_ref, t_ref, base_ref,
    p_ref, last_ref, pc_ref, f_ref, s_ref, ends_ref, carry_ref, hom_ref, x_ref, sems,
):
    copies = [
        pltpu.make_async_copy(plan_hbm.at[:, 512:640, 0:256], last_ref, sems.at[8]),
        pltpu.make_async_copy(plan_hbm.at[:, 640:704, 0:896], pc_ref, sems.at[9]),
    ]

    def fetch(k):
        return pltpu.make_async_copy(
            plan_hbm.at[k, 0:512, 0:640], p_ref.at[k], sems.at[k]
        )

    for copy in copies + [fetch(k) for k in range(8)]:
        copy.start()

    j = lax.axis_index("y") * lax.axis_size("x") + lax.axis_index("x")
    h = lax.axis_index("zh")
    own_block, own_start = j // 2, pl.multiple_of((j % 2) * 128 + h * 64, 64)
    own_low = pl.multiple_of(own_start + 256, 64)

    def block_of(ref, k, start):
        return jnp.concatenate(
            [
                jnp.concatenate(
                    [
                        ref[2 * k + u // 2, u % 2, start + 64 * part : start + 64 * part + 64]
                        for u in range(4)
                    ],
                    axis=0,
                )
                for part in range(2)
            ],
            axis=1,
        )

    def parts(product):
        rows = product.shape[0] // 2
        top, low = product[:rows], product[rows:]
        return top[:, :128] - low[:, 128:], top[:, 128:] + low[:, :128]

    def twice(x):
        return jnp.concatenate([x, x], axis=0)

    def put_end(k, source):
        product = dot(last_ref[k], source)
        real, imag = parts(product[:64] + product[64:])
        high, low = halves(jnp.concatenate([real, imag], axis=1))
        ends_ref[0, k], ends_ref[1, k], ends_ref[2, k] = high, low, high

    def coarse():
        return dot(pc_ref[:, :, 0:768].reshape(512, 768), ends_ref[...].reshape(768, 256))

    def rows_of(product, k):
        part = product[k * 64 : k * 64 + 64]
        return jnp.concatenate(parts(part), axis=1)

    def triple(x):
        high, low = halves(x)
        return jnp.concatenate([high, low, high], axis=0)

    for k in range(8):
        f_ref[k] = block_of(force_ref, k, 0)
    copies[0].wait()
    for k in range(8):
        put_end(k, f_ref[k])
    copies[1].wait()
    initial = jnp.concatenate([lg_ref[0, 0, 0:32], lg_ref[0, 0, 64:96]], axis=1)
    hom = dot(pc_ref[:, :, 768:832].reshape(512, 64), twice(initial))
    carry = coarse() + hom
    hom_ref[0] = carry_ref[0] = triple(initial.astype(f32))
    for k in range(7):
        hom_ref[k + 1] = triple(rows_of(hom, k))
        carry_ref[k + 1] = triple(rows_of(carry, k))
    factor = couplings(coupling_ref[...], 2)

    def piece(k, u):
        n, row = 4 * k + u, u * 64

        width = 128 if u < 2 else 256
        rows = jnp.concatenate(
            [
                jnp.concatenate(
                    [p_ref[k, at : at + 64, lane : lane + width] for lane in (0, 256)]
                    + [p_ref[k, at : at + 64, 512:608]],
                    axis=1,
                )
                for at in (row, row + 256)
            ],
            axis=0,
        )
        force = f_ref[k, 0:width]
        source = jnp.concatenate([force, force, carry_ref[k]], axis=0)
        real, imag = parts(dot(rows, source))
        j_at, h_at = 2 * k + u // 2, u % 2
        g = lg_ref[j_at, h_at, 128:256].astype(f32)
        spectral_re, spectral_im = spectral(real, imag, g[:64], g[64:], factor)
        s = jnp.concatenate([spectral_re, spectral_im], axis=1).astype(bf16)
        s_ref[k, pl.ds(row, 64)] = s
        y_ref[j_at, h_at, 0:64] = real.astype(bf16)
        y_ref[j_at, h_at, 64:128] = imag.astype(bf16)
        x_ref[n, 0:64], x_ref[n, 64:128] = real, imag

    def block(k, _):
        fetch(k).wait()
        for u in range(4):
            piece(k, u)
        return 0

    lax.fori_loop(0, 8, block, 0)
    for k in range(8):
        put_end(k, s_ref[k])
    carry = coarse()
    carry_ref[0] = jnp.zeros((96, 256), bf16)
    for k in range(7):
        carry_ref[k + 1] = triple(rows_of(carry, k))

    def own(ref):
        return jnp.concatenate(
            [ref[own_block, pl.ds(own_start, 64)], ref[own_block, pl.ds(own_low, 64)]], axis=0
        )

    p_own, s_own = own(p_ref), s_ref[own_block]
    source = jnp.concatenate([s_own, s_own, carry_ref[own_block]], axis=0)
    real, imag = parts(dot(p_own[:, 0:608], source))
    t_ref[0:64], t_ref[64:128] = real.astype(bf16), imag.astype(bf16)
    real, imag = parts(dot(p_own[:, 512:608], hom_ref[own_block]))
    base = x_ref[2 * j + h]
    base_ref[0:64] = 0.5 * (base[0:64] + real)
    base_ref[64:128] = 0.5 * (base[64:128] + imag)


PRED_SCRATCH = [
    pltpu.VMEM((8, 512, 640), bf16),
    pltpu.VMEM((8, 128, 256), bf16),
    pltpu.VMEM((8, 64, 896), bf16),
    pltpu.VMEM((8, 256, 256), bf16),
    pltpu.VMEM((8, 256, 256), bf16),
    pltpu.VMEM((3, 8, 32, 256), bf16),
    pltpu.VMEM((8, 96, 256), bf16),
    pltpu.VMEM((8, 96, 256), bf16),
    pltpu.VMEM((32, 128, 128), f32),
    pltpu.SemaphoreType.DMA((10,)),
]


def call(kernel, outs, scratch, ins, flops, moved, grant=24, place=VMEM, flags=None):
    return pl.pallas_call(
        kernel,
        out_shape=outs,
        in_specs=ins,
        out_specs=jax.tree.map(lambda _: place, outs),
        scratch_shapes=scratch,
        compiler_params=pltpu.CompilerParams(vmem_limit_bytes=int(grant * (1 << 20)), flags=flags),
        cost_estimate=pl.CostEstimate(flops=flops, bytes_accessed=moved, transcendentals=0),
    )


def shape(*dims, kind=bf16):
    return jax.ShapeDtypeStruct(dims, kind)


def shards(window, damping, propagator, coupling):
    orbitals = coupling.shape[0]
    horizon = damping.shape[0] * lax.axis_size(FIRST)
    scale = 1.0 / (horizon * math.sqrt(orbitals))
    strength = coupling.reshape(1, 32)
    message = call(
        compose,
        shape(392, 128),
        [],
        [VMEM, VMEM, VMEM],
        40 * 64 * 128,
        400 << 10,
        63.9,
    )(window.reshape(2, 2, 64, 128), damping, strength)
    pair = lax.all_gather(message, "zh")
    lg = from_everyone(pair[:, :264], PLANE)

    s_rows = lax.all_gather(pair[:, 264:], "zm")
    s_rows = lax.all_gather(s_rows, "zq")
    s_other = swapped(s_rows, "c")

    c1 = call(
        functools.partial(first_collision, scale),
        shape(16, 2, 128, 128),
        [pltpu.VMEM((256, 256), f32)],
        [VMEM, VMEM, VMEM],
        2 * 256 * 256 * 2048,
        4 << 20,
    )(s_rows, s_other, lg)
    force = lax.all_to_all(c1, PLANE, 0, 0, tiled=True)

    parts = lg[:, :, 256:258].reshape(64, 128).astype(f32)
    damp = parts[:, 0:32] + (parts[:, 32:64] + parts[:, 64:96])
    damp = jnp.tile(damp.T, (2, 1))
    plan = call(
        build_steps,
        shape(8, 704, 1024),
        [
            pltpu.VMEM((8, 512, 640), bf16),
            pltpu.VMEM((8, 128, 256), bf16),
            pltpu.VMEM((8, 64, 896), bf16),
            pltpu.VMEM((8, 64, 256), f32),
            pltpu.SemaphoreType.DMA((10,)),
        ],
        [VMEM, VMEM],
        64 * 2 * 64 * 256 * 256,
        6 << 20,
        54,
        HBM,
    )(damp, propagator.reshape(64, 32))

    y2, t2, base = call(
        predict,
        (shape(16, 2, 128, 128), shape(128, 128), shape(128, 128, kind=f32)),
        PRED_SCRATCH,
        [VMEM] * 3 + [HBM],
        2 * 8 * 512 * 512 * 128 * 2,
        10 << 20,
        44,
    )(force, lg, strength, plan)

    t_rows = from_everyone(lax.all_gather(t2, "zm"), "zq")
    t_rows = lax.all_gather(t_rows, "c")
    out = call(
        functools.partial(last_collision, scale),
        shape(2, 64, 128, kind=f32),
        [pltpu.VMEM((128, 256), f32)],
        [VMEM, VMEM, VMEM],
        2 * 128 * 256 * 2048,
        2 << 20,
    )(t_rows, y2, base)
    return out.reshape(2, 2, orbitals, 128)


def solution(mesh):
    finer = Mesh(mesh.devices.reshape(4, 4, 2, 2, 4, 2), (*FIRST, *SECOND))
    placed = (P(None, None, FIRST, None, SECOND), P(FIRST, None), P(), P())
    return jax.shard_map(
        shards, mesh=finer, in_specs=placed, out_specs=P(None, FIRST, None, SECOND), check_vma=False
    )
```
